256 devices in a mesh: expert: 8 (over y, core), dp: 32 (over z, x).
Axes of the slice: x: 4, y: 4, z: 8, core: 2. Of those that a mesh axis runs over, the one named last changes fastest.
Arguments:
- tokens: bfloat16 [32768, 3584], P(('expert', 'dp')), may hold values from -6 to 6
- grad_out: bfloat16 [32768, 3584], P(('expert', 'dp')), may hold values from -4 to 4
- route_weights: float32 [32768, 8], P(('expert', 'dp')), may hold values from 0.05 to 0.5
- expert_ids: int32 [32768, 8], P(('expert', 'dp')), may hold values from 0 to 255, all different within a row; in each aligned block of 128 rows (0 to 127, 128 to 255, ...) at most 5 rows name the same one
- swap_code: int32 [8], replicated, may hold values from 0 to 7, as said below
- w_in: bfloat16 [8, 2, 2048, 3584], P('expert', None, 'dp'), may hold values from -0.09375 to 0.09375
- w_down: bfloat16 [8, 2048, 3584], P('expert', 'dp'), may hold values from -0.125 to 0.125
- moment1: float32 [8, 2048, 3584], P('expert', 'dp'), may hold values from -6 to 6
- moment2: float32 [8, 2048, 3584], P('expert', 'dp'), may hold values from 0.05 to 1
Outputs:
- new_down: bfloat16 [8, 2048, 3584], P('expert', 'dp')
- new_moment1: float32 [8, 2048, 3584], P('expert', 'dp')
- new_moment2: float32 [8, 2048, 3584], P('expert', 'dp')
- grad_in: bfloat16 [8, 2, 2048, 3584], P('expert', None, 'dp')
The draws below stay inside these ranges and needn't reach their ends.
Inputs may be any that keep to these rules, and one draw needn't show every extreme that they name: `expert_ids`: each row names 8 different experts; in the rows of one device no expert is named more than 5 times. `swap_code`: entry 0 has all of its 3 low bits set.
All inputs are finite; a program needn't handle non-finite values.
Results may differ from the reference program's by a relative error of at most 0.0057.
Values may be sent and summed in bfloat16 or wider, within the bound.
A program may use at most 128 MiB of HBM per device.

```python
import math
import jax
import jax.numpy as jnp
import numpy as np
from jax import lax

D = 3584
FF = 2048
E_ALL = 256
TOP = 8
TOK_DEV = 128
CAP = 5
EXPERTS = 8
SECTIONS = 3
TOKENS = 32768


def draw_swap_code(key, part):
    codes = jax.random.randint(key, (EXPERTS,), 0, EXPERTS, dtype=jnp.int32)
    return codes.at[0].set(EXPERTS - 1)


def level_of(own_key, extent, shards, least, largest):
    def one(dim, shards_of):
        draws = jax.random.uniform(jax.random.fold_in(jax.random.fold_in(own_key, 6), dim), (shards_of,), jnp.float32, least / len(shards), largest / len(shards))
        return jnp.repeat(jnp.exp(draws), extent[dim] // shards_of).reshape((-1,) + (1,) * (len(extent) - dim - 1))

    loudness = one(*shards[0])
    for cut in shards[1:]:
        loudness = loudness * one(*cut)
    return loudness


def shared_out(own_key, own, number, rows, number_of, top, bound, slope):
    ranking = jax.random.permutation(own_key, number_of)
    heavy_load, ordinary = shares(number_of, rows * top, bound, slope, True), shares(number_of, rows * top, bound, slope, False)
    places = jnp.arange(number_of)

    def named(tallies, offset_by):
        used = int((tallies > 0).sum())
        fixed = max(1, used // 4)
        moved = fixed + (places - fixed + offset_by * (used - fixed)) % max(1, number_of - fixed)
        return jnp.zeros((number_of,), jnp.int32).at[ranking[jnp.where(places < fixed, places, moved)]].set(jnp.asarray(tallies, jnp.int32))

    tallies = jnp.where(number % 4 == 0, named(heavy_load, number // 4), named(ordinary, number - number // 4 - 1))
    mixed = jax.random.permutation(jax.random.fold_in(own, 3), number_of)
    source_of, receiver = mixed[0:number_of // 2 * 2:2], mixed[1:number_of // 2 * 2:2]
    room = jnp.minimum(tallies[source_of] - 1, bound - tallies[receiver]) // 2
    room = jnp.where((source_of == ranking[0]) | (receiver == ranking[0]) | (tallies[receiver] == 0), 0, jnp.maximum(room, 0))
    moved = jax.random.randint(jax.random.fold_in(own, 4), (number_of // 2,), 0, 1 << 20) % (room + 1)
    tallies = tallies.at[source_of].add(-moved).at[receiver].add(moved)
    members = jnp.searchsorted(jnp.cumsum(tallies), jnp.arange(rows * top), side="right").astype(jnp.int32)
    listing = members.reshape(top, rows).T
    listing = listing[jax.random.permutation(jax.random.fold_in(own, 1), rows)]
    offset_by = jax.random.randint(jax.random.fold_in(own, 2), (rows, 1), 0, top)
    return jnp.take_along_axis(listing, (jnp.arange(top)[None, :] + offset_by) % top, axis=1)


def shares(amount, total, limit, skew, full):
    loads = [(1 << 20) // math.isqrt(rank ** skew) + 1 for rank in range(1, amount + 1)]
    largest = limit if full else min(limit, max(-(-total // amount), total * loads[0] // sum(loads)))
    least = 1 if total - largest >= amount - 1 else 0
    counts, rest = [largest] + [least] * (amount - 1), total - largest - least * (amount - 1)
    while rest > 0:
        candidates = [i for i in range(1, amount) if counts[i] < largest] or [i for i in range(1, amount) if counts[i] < limit]
        pool, left = sum([loads[i] for i in candidates]), rest
        for i in candidates:
            extra = min(limit - counts[i], max(1, left * loads[i] // pool), rest)
            counts[i] = counts[i] + extra
            rest = rest - extra
    return np.array(counts)


def noise(own_key, extent, scale, reach, shards=(), kind=jnp.bfloat16):
    loudness = level_of(own_key, extent, shards, -0.22, 0.18) if shards else 1.0
    result = jax.random.normal(own_key, extent, jnp.float32) * scale * loudness
    return jnp.minimum(jnp.maximum(result, -reach), reach).astype(kind)


def setup_inputs(seed: int = 0) -> dict:
    key_list = jax.random.split(jax.random.key(seed), 10)
    tokens = noise(key_list[0], (TOKENS, D), 1.0, 6.0, ((0, 256),))
    grad_out = noise(key_list[1], (TOKENS, D), 0.3, 4.0, ((0, 256),))
    route_weights = jnp.clip(jnp.exp(math.log(0.5) - 2.3025851 * jax.random.uniform(key_list[2], (TOKENS, TOP), jnp.float32) ** level_of(key_list[2], (TOKENS, TOP), ((0, 256),), -0.2, 0.2)), 0.05, 0.5)
    expert_ids_keys = jax.random.split(jax.random.fold_in(key_list[3], 1), TOKENS // TOK_DEV)
    expert_ids_turns = jax.random.permutation(jax.random.fold_in(key_list[3], 3), TOKENS // TOK_DEV)
    expert_ids = jax.vmap(lambda own, number: shared_out(jax.random.fold_in(key_list[3], 2), own, number, TOK_DEV, E_ALL, TOP, CAP, 1))(expert_ids_keys, expert_ids_turns).reshape((TOKENS, TOP))
    swap_code = draw_swap_code(jax.random.fold_in(key_list[9], 71), 0)
    w_in = noise(key_list[5], (EXPERTS, 2, FF, D), D ** -0.5, 0.09375, ((0, 8), (2, 32)))
    w_down = noise(key_list[6], (EXPERTS, FF, D), FF ** -0.5, 0.125, ((0, 8), (1, 32)))
    moment1 = noise(key_list[7], (EXPERTS, FF, D), 1.0, 6.0, ((0, 8), (1, 32)), jnp.float32)
    moment2 = jnp.clip(jnp.exp(math.log(1.0) - 2.9957323 * jax.random.uniform(key_list[8], (EXPERTS, FF, D), jnp.float32) ** level_of(key_list[8], (EXPERTS, FF, D), ((0, 8), (1, 32)), -0.2, 0.2)), 0.05, 1.0)
    return dict(tokens=tokens, grad_out=grad_out, route_weights=route_weights, expert_ids=expert_ids, swap_code=swap_code, w_in=w_in, w_down=w_down, moment1=moment1, moment2=moment2)


adam_rate = 0.01
beta_one = 0.9
beta_two = 0.999
adam_step = 100.0
adam_eps = 1e-08

def contract(left_side, right_side, left_dim, right_dim):
    return lax.dot_general(left_side, right_side, (((left_dim,), (right_dim,)), ((), ())), preferred_element_type=jnp.float32)

def forward_rows(token_rows, w_gate, w_up):
    gate_proj = contract(token_rows, w_gate, 1, 1)
    up_proj = contract(token_rows, w_up, 1, 1)
    sigmoid_val = jax.nn.sigmoid(gate_proj)
    activated = gate_proj * sigmoid_val
    slopes = sigmoid_val * (1.0 + gate_proj * (1.0 - sigmoid_val))
    hidden = (activated * up_proj).astype(jnp.bfloat16)
    return (up_proj, activated, slopes, hidden)

def backward_rows(token_rows, grad_rows, up_proj, activated, slopes, hidden, w_dn):
    back_grad = contract(grad_rows, w_dn, 1, 1)
    gate_back = (back_grad * up_proj * slopes).astype(jnp.bfloat16)
    up_back = (back_grad * activated).astype(jnp.bfloat16)
    return (contract(hidden, grad_rows, 0, 0), contract(gate_back, token_rows, 0, 0), contract(up_back, token_rows, 0, 0))

def slot_order(swap_code):
    slot_ids = jnp.arange(EXPERTS, dtype=jnp.int32)
    source = slot_ids
    for section_bit in range(SECTIONS):
        partner_slot = jnp.bitwise_xor(slot_ids, 1 << section_bit)
        lower_slot = jnp.minimum(slot_ids, partner_slot)
        swapped = swap_code[lower_slot] // (1 << section_bit) % 2 == 1
        source = source[jnp.where(swapped, partner_slot, slot_ids)]
    return source

def reference(tokens, grad_out, route_weights, expert_ids, swap_code, w_in, w_down, moment1, moment2):
    most_rows = CAP * (TOKENS // TOK_DEV)
    row_ids = jnp.arange(most_rows, dtype=jnp.int32)

    def one_expert(packed):
        expert, weight_in, weight_down = packed
        hits = expert_ids == expert
        picked = jnp.any(hits, axis=1)
        row_scale = lax.optimization_barrier(jnp.sum(jnp.where(hits, route_weights, 0.0), axis=1))
        chosen = jnp.nonzero(picked, size=most_rows, fill_value=0)[0].astype(jnp.int32)
        filled = row_ids < jnp.sum(picked.astype(jnp.int32))
        token_rows = jnp.where(filled[:, None], tokens[chosen], jnp.zeros((), tokens.dtype))
        weights_used = jnp.where(filled, row_scale[chosen], 0.0)
        grad_rows = (grad_out[chosen].astype(jnp.float32) * weights_used[:, None]).astype(jnp.bfloat16)
        up_proj, activated, slopes, hidden = forward_rows(token_rows, weight_in[0], weight_in[1])
        down_grad, gate_grad, up_grad = backward_rows(token_rows, grad_rows, up_proj, activated, slopes, hidden, weight_down)
        return (down_grad, jnp.stack([gate_grad, up_grad]))
    down_grad, in_grad = lax.map(one_expert, (jnp.arange(EXPERTS, dtype=jnp.int32), w_in, w_down))
    first_new = beta_one * moment1 + (1.0 - beta_one) * down_grad
    second_new = beta_two * moment2 + (1.0 - beta_two) * down_grad * down_grad
    fix_one = 1.0 - beta_one ** adam_step
    fix_two = 1.0 - beta_two ** adam_step
    step_size = first_new / fix_one / (jnp.sqrt(second_new / fix_two) + adam_eps)
    updated = (w_down.astype(jnp.float32) - adam_rate * step_size).astype(jnp.bfloat16)
    source = slot_order(swap_code)
    return (updated[source], first_new[source], second_new[source], in_grad.astype(jnp.bfloat16)[source])
```

```python
import functools
import heapq

import jax
import jax.numpy as jnp
from jax import lax
from jax.experimental import pallas as pl
from jax.experimental.pallas import tpu as pltpu
from jax.sharding import PartitionSpec as P

CAP = 5
ADAM_RATE = 0.01
BETA_ONE = 0.9
BETA_TWO = 0.999
ADAM_STEP = 100.0
ADAM_EPS = 1e-08
NX, NZ = 4, 8
NE = 8
ROWS_A, ROWS_B = 32, 48
PAIRS_A, PAIRS_B = ROWS_A // 2, ROWS_B // 2
F32, BF16 = jnp.float32, jnp.bfloat16
STREAMS = {"xM": (1, 0), "xm": (-1, 0), "zM": (0, 1), "zm": (0, -1)}


def forwards(item):
    color, kx, kz = item
    ring_x = (["xM"] if 0 <= kx < NX // 2 else []) + (["xm"] if 1 - NX // 2 < kx <= 0 else [])
    ring_z = (["zM"] if 0 <= kz < NZ // 2 else []) + (["zm"] if 1 - NZ // 2 < kz <= 0 else [])
    if color == "B":
        return ring_z + ["xM", "xm"] if kx == 0 else ring_x
    return ring_x + ["zM", "zm"] if kz == 0 else ring_z


def plan():
    free = dict.fromkeys(STREAMS, 0.0)
    queue, log, number = [], [], 0

    def send(now, item):
        nonlocal number
        for stream in forwards(item):
            free[stream] = max(free[stream], now) + (ROWS_A if item[0] == "A" else ROWS_B)
            dx, dz = STREAMS[stream]
            number += 1
            heapq.heappush(queue, (free[stream] + 8, number, (item[0], item[1] + dx, item[2] + dz)))

    send(0, ("B", 0, 0))
    send(0, ("A", 0, 0))
    while queue:
        now, _, item = heapq.heappop(queue)
        log.append((now, item))
        send(now, item)
    return log


PLAN = plan()
N_SENDS = len(PLAN)


def kernel(
    ids_ref, route_ref, swap_ref, tok_hbm, grad_hbm, win_hbm, wdn_hbm, mom1_hbm, mom2_hbm,
    gin_out, dgrad_out, wdn_out, mom1_out, mom2_out,
    tok, gout, mom, sel_t, sel_g, scale, hits, send, recv, block_a, block_b,
    stage, spread_w, spread_m, again_w, again_m, weights, moments, acc, gin,
    load_sem, out_sem, self_sem, disp_s, disp_r, w1_s, w1_r, w2_s, w2_r, m1_s, m1_r, m2_s, m2_r, a_r, b_r, ab_s,
):
    width = tok.shape[1]
    hidden = 64
    me = lax.axis_index("expert")
    dp = lax.axis_index("dp")
    z, x = dp // NX, lax.rem(dp, NX)
    sign = 1 - 2 * lax.rem(me, 2)

    loads = [
        pltpu.make_async_copy(tok_hbm, tok, load_sem.at[0]),
        pltpu.make_async_copy(grad_hbm, gout, load_sem.at[1]),
        pltpu.make_async_copy(win_hbm.at[0, 0], stage.at[pl.ds(0, hidden)], load_sem.at[2]),
        pltpu.make_async_copy(win_hbm.at[0, 1], stage.at[pl.ds(hidden, hidden)], load_sem.at[3]),
        pltpu.make_async_copy(wdn_hbm.at[0], stage.at[pl.ds(2 * hidden, hidden)], load_sem.at[4]),
        pltpu.make_async_copy(mom1_hbm.at[0], mom.at[0], load_sem.at[5]),
        pltpu.make_async_copy(mom2_hbm.at[0], mom.at[1], load_sem.at[6]),
    ]
    for copy in loads:
        copy.start()

    def at_x(step):
        return lax.rem(x + NX - sign * step + NX, NX)

    def at_z(step):
        return lax.rem(z + NZ - sign * step, NZ)

    target = {
        "xM": (me, z * NX + at_x(-1)),
        "xm": (me, z * NX + at_x(1)),
        "zM": (me, at_z(-1) * NX + x),
        "zm": (me, at_z(1) * NX + x),
    }
    peers = [(lax.rem(me + i, NE), dp) for i in range(1, NE)]
    barrier = pltpu.get_barrier_semaphore()
    everyone = peers + list(target.values())
    for device in everyone:
        pl.semaphore_signal(barrier, inc=1, device_id=device, device_id_type=pl.DeviceIdType.MESH)

    order = [jnp.int32(s) for s in range(NE)]
    for bit in range(3):
        taken = []
        for s in range(NE):
            partner = s ^ (1 << bit)
            code = swap_ref[min(s, partner)]
            swapped = lax.rem(lax.div(code, jnp.int32(1 << bit)), jnp.int32(2)) == 1
            taken.append(jnp.where(swapped, order[partner], order[s]))
        order = taken

    ids = ids_ref[...]
    route = route_ref[...]
    count = ids.shape[1]
    weight_rows = []
    for s in range(NE):
        match = ids == order[s]
        hits[s : s + 1, :] = jnp.max(jnp.where(match, 1.0, 0.0), axis=0, keepdims=True)
        weight_rows.append(jnp.sum(jnp.where(match, route, 0.0), axis=0, keepdims=True))
    earlier = lax.broadcasted_iota(jnp.int32, (count, count), 0) < lax.broadcasted_iota(jnp.int32, (count, count), 1)
    hit = hits[...]
    rank = jnp.dot(hit.astype(BF16), jnp.where(earlier, 1.0, 0.0).astype(BF16), preferred_element_type=F32)
    row16 = lax.broadcasted_iota(jnp.int32, (16, count), 0)
    row8 = lax.rem(row16, 8).astype(F32)
    first = row16 < 8
    for s in range(NE):
        chosen = jnp.where((rank[s : s + 1, :] == row8) & (hit[s : s + 1, :] > 0.5), 1.0, 0.0)
        sel_t[16 * s : 16 * s + 16, :] = jnp.where(first, chosen, 0.0).astype(BF16)
        sel_g[16 * s : 16 * s + 16, :] = jnp.where(first, 0.0, chosen).astype(BF16)
        scaled = jnp.sum(chosen * weight_rows[s], axis=1, keepdims=True)
        scale[16 * s : 16 * s + 16, :] = jnp.where(
            lax.broadcasted_iota(jnp.int32, (16, 1), 0) < 8, 1.0, scaled
        )
    loads[0].wait()
    loads[1].wait()
    tile = 512

    def select(i, carry):
        columns = pl.ds(pl.multiple_of(i * tile, tile), tile)
        rows = jnp.dot(sel_t[...], tok[:, columns], preferred_element_type=F32)
        rows += jnp.dot(sel_g[...], gout[:, columns], preferred_element_type=F32)
        send[:, :, columns] = (rows * scale[...]).astype(BF16).reshape(NE, 16, tile)
        return carry

    lax.fori_loop(0, width // tile, select, 0)
    pl.semaphore_wait(barrier, len(everyone))

    def remote(src, dst, send_sem, recv_sem, device):
        return pltpu.make_async_remote_copy(
            src_ref=src, dst_ref=dst, send_sem=send_sem, recv_sem=recv_sem,
            device_id=device, device_id_type=pl.DeviceIdType.MESH,
        )

    pending = []

    def exchange(src_of, dst_of, send_sems, recv_sems, own_sem):
        copies = []
        for i in range(1, NE):
            k = lax.rem(me + i, NE)
            copy = remote(src_of(k), dst_of(me), send_sems.at[i], recv_sems.at[i], (k, dp))
            copy.start()
            copies.append(copy)
        own = pltpu.make_async_copy(src_of(me), dst_of(me), own_sem)
        own.start()
        pending.extend(copies)

        def wait():
            own.wait()
            for i in range(1, NE):
                k = lax.rem(me + NE - i, NE)
                remote(src_of(k), dst_of(k), send_sems.at[i], recv_sems.at[i], (k, dp)).wait_recv()

        return wait

    wait_dispatch = exchange(
        lambda k: send.at[k], lambda k: recv.at[k], disp_s, disp_r, self_sem.at[0]
    )
    for copy in loads[2:]:
        copy.wait()
    stage[3 * hidden : 4 * hidden, :] = mom[0].astype(BF16)
    stage[4 * hidden : 5 * hidden, :] = mom[1].astype(BF16)
    acc[...] = jnp.zeros_like(acc)
    wait_dispatch()

    lanes = lax.broadcasted_iota(jnp.int32, (ROWS_A + ROWS_B, NE * 16), 1)
    lines = lax.broadcasted_iota(jnp.int32, (ROWS_A + ROWS_B, NE * 16), 0)
    in_b = lines >= ROWS_A
    local_line = jnp.where(in_b, lines - ROWS_A, lines)
    pairs = jnp.where(in_b, PAIRS_B, PAIRS_A)
    is_grad = local_line >= pairs
    pair = jnp.where(is_grad, local_line - pairs, local_line) + jnp.where(in_b, PAIRS_A, 0)
    wanted = lax.div(pair, CAP) * 16 + lax.rem(pair, CAP) + jnp.where(is_grad, 8, 0)
    compact = jnp.where(lanes == wanted, 1.0, 0.0).astype(BF16)

    def pack(i, carry):
        columns = pl.ds(pl.multiple_of(i * tile, tile), tile)
        rows = jnp.dot(compact, recv[:, :, columns].reshape(NE * 16, tile), preferred_element_type=F32)
        rows = rows.astype(BF16)
        block_a[z, x, :, columns] = rows[:ROWS_A]
        block_b[z, x, :, columns] = rows[ROWS_A:]
        return carry

    lax.fori_loop(0, width // tile, pack, 0)

    sent = 0

    def sem_of(item):
        color, kx, kz = item
        return (a_r if color == "A" else b_r).at[(kz + NZ // 2 - 1) * NX + kx + NX // 2 - 1]

    def slot_of(item):
        color, kx, kz = item
        return (block_a if color == "A" else block_b).at[at_z(kz), at_x(kx)]

    def pass_on(item):
        nonlocal sent
        for stream in forwards(item):
            dx, dz = STREAMS[stream]
            there = (item[0], item[1] + dx, item[2] + dz)
            copy = remote(slot_of(item), slot_of(item), ab_s.at[sent], sem_of(there), target[stream])
            copy.start()
            pending.append(copy)
            sent += 1

    def receive(item):
        remote(slot_of(item), slot_of(item), ab_s.at[0], sem_of(item), target["xM"]).wait_recv()

    def compute(color, kz):
        block, n_pairs = (block_a, PAIRS_A) if color == "A" else (block_b, PAIRS_B)
        rows = NX * 2 * n_pairs
        at = at_z(kz)

        def forward(i, total):
            columns = pl.ds(pl.multiple_of(i * tile, tile), tile)
            return total + lax.dot_general(
                block[at, :, :, columns].reshape(rows, tile), weights[:, columns],
                (((1,), (1,)), ((), ())), preferred_element_type=F32,
            )

        made = lax.fori_loop(0, width // tile, forward, jnp.zeros((rows, 4 * hidden), F32))
        made = made.reshape(NX, 2, n_pairs, 4 * hidden)
        both = made[:, 0, :, : 2 * hidden].reshape(NX * n_pairs, 2 * hidden)
        back = made[:, 1, :, 2 * hidden :].reshape(NX * n_pairs, 2 * hidden)
        turned = pltpu.roll(both, hidden, 1)
        low = lax.broadcasted_iota(jnp.int32, both.shape, 1) < hidden
        gate = jnp.where(low, both, turned)
        up = jnp.where(low, turned, both)
        sg = jax.nn.sigmoid(gate)
        act = gate * sg
        grads = jnp.where(low, back * up * (sg * (1.0 + gate * (1.0 - sg))), back * act)
        hid = jnp.where(low, act * up, 0.0)
        grads = grads.reshape(NX, 1, n_pairs, 2 * hidden)
        hid = hid.reshape(NX, 1, n_pairs, 2 * hidden)
        nothing = jnp.zeros_like(hid)
        left = jnp.concatenate(
            [
                jnp.concatenate([grads, nothing], axis=1).reshape(rows, 2 * hidden),
                jnp.concatenate([nothing, hid], axis=1).reshape(rows, 2 * hidden),
            ],
            axis=1,
        )
        left = left.T.astype(BF16)

        def backward(i, carry):
            columns = pl.ds(pl.multiple_of(i * tile, tile), tile)
            acc[:, columns] += jnp.dot(
                left, block[at, :, :, columns].reshape(rows, tile), preferred_element_type=F32
            )
            return carry

        lax.fori_loop(0, width // tile, backward, 0)

    quarter = width // 4
    half_w, half_m = 3 * hidden // 2, hidden

    def slice_w(ref, base):
        return lambda k: ref.at[
            pl.ds(pl.multiple_of(base + half_w * lax.rem(k, 2), 16), half_w),
            pl.ds(pl.multiple_of(quarter * lax.div(k, 2), 128), quarter),
        ]

    def slice_m(ref, base):
        return lambda k: ref.at[
            pl.ds(pl.multiple_of(base + half_m * lax.rem(k, 2), 16), half_m),
            pl.ds(pl.multiple_of(quarter * lax.div(k, 2), 128), quarter),
        ]

    pass_on(("B", 0, 0))
    pass_on(("A", 0, 0))
    waits = {}
    have = {}
    ready = []
    state = {"weights": False}

    def step_spread():
        waits["w1"] = exchange(slice_w(stage, 0), lambda k: spread_w.at[k], w1_s, w1_r, self_sem.at[1])
        waits["m1"] = exchange(slice_m(stage, 3 * hidden), lambda k: spread_m.at[k], m1_s, m1_r, self_sem.at[3])

    def step_gather_w():
        waits["w1"]()
        for s in range(NE):
            again_w[s, :, :] = spread_w[order[s]]
        waits["w2"] = exchange(lambda k: again_w.at[k], slice_w(weights, 0), w2_s, w2_r, self_sem.at[2])

    def step_gather_m():
        waits["m1"]()
        for s in range(NE):
            again_m[s, :, :] = spread_m[order[s]]
        waits["m2"] = exchange(lambda k: again_m.at[k], slice_m(moments, 0), m2_s, m2_r, self_sem.at[4])

    def step_weights():
        waits["w2"]()
        weights[3 * hidden : 4 * hidden, :] = weights[2 * hidden : 3 * hidden, :]
        state["weights"] = True

    step_spread()
    last = PLAN[-1][0]
    steps = [(0.25, step_gather_w), (0.36, step_gather_m), (0.5, step_weights)]
    have = {("A", 0): 1, ("B", 0): 1}
    for when, item in PLAN:
        while steps and when >= steps[0][0] * last:
            steps.pop(0)[1]()
        receive(item)
        pass_on(item)
        key = (item[0], item[2])
        have[key] = have.get(key, 0) + 1
        if have[key] == NX:
            ready.append(key)
        if state["weights"] and ready:
            compute(*ready.pop(0))
    for key in ready:
        compute(*key)
    waits["m2"]()

    gin[...] = acc[: 2 * hidden, :].astype(BF16)
    outs = [
        pltpu.make_async_copy(acc.at[pl.ds(2 * hidden, hidden)], dgrad_out, out_sem.at[0]),
        pltpu.make_async_copy(gin, gin_out, out_sem.at[1]),
        pltpu.make_async_copy(weights.at[pl.ds(2 * hidden, hidden)], wdn_out, out_sem.at[2]),
        pltpu.make_async_copy(moments.at[pl.ds(0, hidden)], mom1_out, out_sem.at[3]),
        pltpu.make_async_copy(moments.at[pl.ds(hidden, hidden)], mom2_out, out_sem.at[4]),
    ]
    for copy in outs:
        copy.start()
    for copy in pending:
        copy.wait_send()
    for copy in outs:
        copy.wait()


def local(tokens, grad_out, route_weights, expert_ids, swap_code, w_in, w_down, moment1, moment2):
    width = tokens.shape[1]
    hidden = w_down.shape[1]
    vmem, anywhere = pltpu.VMEM, pl.BlockSpec(memory_space=pl.ANY)
    half_w, half_m, quarter = 3 * hidden // 2, hidden, width // 4
    dma = pltpu.SemaphoreType.DMA
    gin, dgrad, wdn, mom1, mom2 = pl.pallas_call(
        kernel,
        out_shape=(
            jax.ShapeDtypeStruct((2 * hidden, width), BF16),
            jax.ShapeDtypeStruct((hidden, width), F32),
            jax.ShapeDtypeStruct((hidden, width), BF16),
            jax.ShapeDtypeStruct((hidden, width), BF16),
            jax.ShapeDtypeStruct((hidden, width), BF16),
        ),
        in_specs=[
            pl.BlockSpec(memory_space=pltpu.VMEM),
            pl.BlockSpec(memory_space=pltpu.VMEM),
            pl.BlockSpec(memory_space=pltpu.SMEM),
        ]
        + [anywhere] * 6,
        out_specs=(anywhere,) * 5,
        scratch_shapes=[
            vmem(tokens.shape, BF16),
            vmem(tokens.shape, BF16),
            vmem((2, hidden, width), F32),
            vmem((16 * NE, tokens.shape[0]), BF16),
            vmem((16 * NE, tokens.shape[0]), BF16),
            vmem((16 * NE, 1), F32),
            vmem((NE, tokens.shape[0]), F32),
            vmem((NE, 16, width), BF16),
            vmem((NE, 16, width), BF16),
            vmem((NZ, NX, ROWS_A, width), BF16),
            vmem((NZ, NX, ROWS_B, width), BF16),
            vmem((5 * hidden, width), BF16),
            vmem((NE, half_w, quarter), BF16),
            vmem((NE, half_m, quarter), BF16),
            vmem((NE, half_w, quarter), BF16),
            vmem((NE, half_m, quarter), BF16),
            vmem((4 * hidden, width), BF16),
            vmem((2 * hidden, width), BF16),
            vmem((4 * hidden, width), F32),
            vmem((2 * hidden, width), BF16),
            dma((7,)), dma((5,)), dma((5,)),
            dma((NE,)), dma((NE,)), dma((NE,)), dma((NE,)), dma((NE,)),
            dma((NE,)), dma((NE,)), dma((NE,)), dma((NE,)), dma((NE,)),
            dma((NX * NZ,)), dma((NX * NZ,)), dma((N_SENDS,)),
        ],
        compiler_params=pltpu.CompilerParams(
            collective_id=0, has_side_effects=True, vmem_limit_bytes=60 << 20
        ),
    )(expert_ids.T, route_weights.T, swap_code, tokens, grad_out, w_in, w_down, moment1, moment2)
    first_new = BETA_ONE * mom1.astype(F32) + (1.0 - BETA_ONE) * dgrad
    second_new = BETA_TWO * mom2.astype(F32) + (1.0 - BETA_TWO) * (dgrad * dgrad)
    fix_one = 1.0 - BETA_ONE**ADAM_STEP
    fix_two = 1.0 - BETA_TWO**ADAM_STEP
    step_size = first_new / fix_one / (jnp.sqrt(second_new / fix_two) + ADAM_EPS)
    down_new = (wdn.astype(F32) - ADAM_RATE * step_size).astype(BF16)
    return down_new[None], first_new[None], second_new[None], gin.reshape(1, 2, hidden, width)


def solution(mesh):
    rows = P(("expert", "dp"), None)
    wide = P("expert", None, "dp", None)
    slot = P("expert", "dp", None)
    return jax.shard_map(
        local,
        mesh=mesh,
        in_specs=(rows, rows, rows, rows, P(), wide, slot, slot, slot),
        out_specs=(slot, slot, slot, wide),
        check_vma=False,
    )
```

```python
import functools
import heapq

import jax
import jax.numpy as jnp
from jax import lax
from jax.experimental import pallas as pl
from jax.experimental.pallas import tpu as pltpu
from jax.sharding import PartitionSpec as P

CAP = 5
ADAM_RATE = 0.01
BETA_ONE = 0.9
BETA_TWO = 0.999
ADAM_STEP = 100.0
ADAM_EPS = 1e-08
NX, NZ = 4, 8
NE = 8
ROWS_A, ROWS_B = 32, 48
PAIRS_A, PAIRS_B = ROWS_A // 2, ROWS_B // 2
F32, BF16 = jnp.float32, jnp.bfloat16
STREAMS = {"xM": (1, 0), "xm": (-1, 0), "zM": (0, 1), "zm": (0, -1)}


def forwards(item):
    color, kx, kz = item
    ring_x = (["xM"] if 0 <= kx < NX // 2 else []) + (["xm"] if 1 - NX // 2 < kx <= 0 else [])
    ring_z = (["zM"] if 0 <= kz < NZ // 2 else []) + (["zm"] if 1 - NZ // 2 < kz <= 0 else [])
    if color == "B":
        return ring_z + ["xM", "xm"] if kx == 0 else ring_x
    return ring_x + ["zM", "zm"] if kz == 0 else ring_z


def plan():
    free = dict.fromkeys(STREAMS, 0.0)
    queue, log, number = [], [], 0

    def send(now, item):
        nonlocal number
        for stream in forwards(item):
            free[stream] = max(free[stream], now) + (ROWS_A if item[0] == "A" else ROWS_B)
            dx, dz = STREAMS[stream]
            number += 1
            heapq.heappush(queue, (free[stream] + 8, number, (item[0], item[1] + dx, item[2] + dz)))

    send(0, ("B", 0, 0))
    send(0, ("A", 0, 0))
    while queue:
        now, _, item = heapq.heappop(queue)
        log.append((now, item))
        send(now, item)
    return log


PLAN = plan()
N_SENDS = len(PLAN)


def kernel(
    ids_ref, route_ref, swap_ref, tok_hbm, grad_hbm, win_hbm, wdn_hbm, mom1_hbm, mom2_hbm,
    gin_out, dgrad_out, wdn_out, mom1_out, mom2_out,
    tok, gout, mom, sel_t, sel_g, scale, hits, send, recv, block_a, block_b,
    stage, spread_w, spread_m, again_w, again_m, weights, weights_t, moments, acc, gin,
    load_sem, out_sem, self_sem, disp_s, disp_r, w1_s, w1_r, w2_s, w2_r, m1_s, m1_r, m2_s, m2_r, a_r, b_r, ab_s,
):
    width = tok.shape[1]
    hidden = 64
    me = lax.axis_index("expert")
    dp = lax.axis_index("dp")
    z, x = dp // NX, lax.rem(dp, NX)
    sign = 1 - 2 * lax.rem(me, 2)

    loads = [
        pltpu.make_async_copy(tok_hbm, tok, load_sem.at[0]),
        pltpu.make_async_copy(grad_hbm, gout, load_sem.at[1]),
        pltpu.make_async_copy(win_hbm.at[0, 0], stage.at[pl.ds(0, hidden)], load_sem.at[2]),
        pltpu.make_async_copy(win_hbm.at[0, 1], stage.at[pl.ds(hidden, hidden)], load_sem.at[3]),
        pltpu.make_async_copy(wdn_hbm.at[0], stage.at[pl.ds(2 * hidden, hidden)], load_sem.at[4]),
        pltpu.make_async_copy(mom1_hbm.at[0], mom.at[0], load_sem.at[5]),
        pltpu.make_async_copy(mom2_hbm.at[0], mom.at[1], load_sem.at[6]),
    ]
    for copy in loads:
        copy.start()

    def at_x(step):
        return lax.rem(x + NX - sign * step + NX, NX)

    def at_z(step):
        return lax.rem(z + NZ - sign * step, NZ)

    target = {
        "xM": (me, z * NX + at_x(-1)),
        "xm": (me, z * NX + at_x(1)),
        "zM": (me, at_z(-1) * NX + x),
        "zm": (me, at_z(1) * NX + x),
    }
    peers = [(lax.rem(me + i, NE), dp) for i in range(1, NE)]
    barrier = pltpu.get_barrier_semaphore()
    everyone = peers + list(target.values())
    for device in everyone:
        pl.semaphore_signal(barrier, inc=1, device_id=device, device_id_type=pl.DeviceIdType.MESH)

    order = [jnp.int32(s) for s in range(NE)]
    for bit in range(3):
        taken = []
        for s in range(NE):
            partner = s ^ (1 << bit)
            code = swap_ref[min(s, partner)]
            swapped = lax.rem(lax.div(code, jnp.int32(1 << bit)), jnp.int32(2)) == 1
            taken.append(jnp.where(swapped, order[partner], order[s]))
        order = taken

    ids = ids_ref[...]
    route = route_ref[...]
    count = ids.shape[1]
    weight_rows = []
    for s in range(NE):
        match = ids == order[s]
        hits[s : s + 1, :] = jnp.max(jnp.where(match, 1.0, 0.0), axis=0, keepdims=True)
        weight_rows.append(jnp.sum(jnp.where(match, route, 0.0), axis=0, keepdims=True))
    earlier = lax.broadcasted_iota(jnp.int32, (count, count), 0) < lax.broadcasted_iota(jnp.int32, (count, count), 1)
    hit = hits[...]
    rank = jnp.dot(hit.astype(BF16), jnp.where(earlier, 1.0, 0.0).astype(BF16), preferred_element_type=F32)
    row16 = lax.broadcasted_iota(jnp.int32, (16, count), 0)
    row8 = lax.rem(row16, 8).astype(F32)
    first = row16 < 8
    for s in range(NE):
        chosen = jnp.where((rank[s : s + 1, :] == row8) & (hit[s : s + 1, :] > 0.5), 1.0, 0.0)
        sel_t[16 * s : 16 * s + 16, :] = jnp.where(first, chosen, 0.0).astype(BF16)
        sel_g[16 * s : 16 * s + 16, :] = jnp.where(first, 0.0, chosen).astype(BF16)
        scaled = jnp.sum(chosen * weight_rows[s], axis=1, keepdims=True)
        scale[16 * s : 16 * s + 16, :] = jnp.where(
            lax.broadcasted_iota(jnp.int32, (16, 1), 0) < 8, 1.0, scaled
        )
    loads[0].wait()
    loads[1].wait()
    tile = 512

    def select(i, carry):
        columns = pl.ds(pl.multiple_of(i * tile, tile), tile)
        rows = jnp.dot(sel_t[...], tok[:, columns], preferred_element_type=F32)
        rows += jnp.dot(sel_g[...], gout[:, columns], preferred_element_type=F32)
        send[:, :, columns] = (rows * scale[...]).astype(BF16).reshape(NE, 16, tile)
        return carry

    lax.fori_loop(0, width // tile, select, 0)
    pl.semaphore_wait(barrier, len(everyone))

    def remote(src, dst, send_sem, recv_sem, device):
        return pltpu.make_async_remote_copy(
            src_ref=src, dst_ref=dst, send_sem=send_sem, recv_sem=recv_sem,
            device_id=device, device_id_type=pl.DeviceIdType.MESH,
        )

    pending = []

    def exchange(src_of, dst_of, send_sems, recv_sems, own_sem):
        copies = []
        for i in range(1, NE):
            k = lax.rem(me + i, NE)
            copy = remote(src_of(k), dst_of(me), send_sems.at[i], recv_sems.at[i], (k, dp))
            copy.start()
            copies.append(copy)
        own = pltpu.make_async_copy(src_of(me), dst_of(me), own_sem)
        own.start()
        pending.extend(copies)

        def wait():
            own.wait()
            for i in range(1, NE):
                k = lax.rem(me + NE - i, NE)
                remote(src_of(k), dst_of(k), send_sems.at[i], recv_sems.at[i], (k, dp)).wait_recv()

        return wait

    wait_dispatch = exchange(
        lambda k: send.at[k], lambda k: recv.at[k], disp_s, disp_r, self_sem.at[0]
    )
    for copy in loads[2:]:
        copy.wait()
    stage[3 * hidden : 4 * hidden, :] = mom[0].astype(BF16)
    stage[4 * hidden : 5 * hidden, :] = mom[1].astype(BF16)
    acc[...] = jnp.zeros_like(acc)
    wait_dispatch()

    lanes = lax.broadcasted_iota(jnp.int32, (ROWS_A + ROWS_B, NE * 16), 1)
    lines = lax.broadcasted_iota(jnp.int32, (ROWS_A + ROWS_B, NE * 16), 0)
    in_b = lines >= ROWS_A
    local_line = jnp.where(in_b, lines - ROWS_A, lines)
    pairs = jnp.where(in_b, PAIRS_B, PAIRS_A)
    is_grad = local_line >= pairs
    pair = jnp.where(is_grad, local_line - pairs, local_line) + jnp.where(in_b, PAIRS_A, 0)
    wanted = lax.div(pair, CAP) * 16 + lax.rem(pair, CAP) + jnp.where(is_grad, 8, 0)
    compact = jnp.where(lanes == wanted, 1.0, 0.0).astype(BF16)

    def pack(i, carry):
        columns = pl.ds(pl.multiple_of(i * tile, tile), tile)
        rows = jnp.dot(compact, recv[:, :, columns].reshape(NE * 16, tile), preferred_element_type=F32)
        rows = rows.astype(BF16)
        block_a[z, x, :, columns] = rows[:ROWS_A]
        block_b[z, x, :, columns] = rows[ROWS_A:]
        return carry

    lax.fori_loop(0, width // tile, pack, 0)

    sent = 0

    def sem_of(item):
        color, kx, kz = item
        return (a_r if color == "A" else b_r).at[(kz + NZ // 2 - 1) * NX + kx + NX // 2 - 1]

    def slot_of(item):
        color, kx, kz = item
        return (block_a if color == "A" else block_b).at[at_z(kz), at_x(kx)]

    def pass_on(item):
        nonlocal sent
        for stream in forwards(item):
            dx, dz = STREAMS[stream]
            there = (item[0], item[1] + dx, item[2] + dz)
            copy = remote(slot_of(item), slot_of(item), ab_s.at[sent], sem_of(there), target[stream])
            copy.start()
            pending.append(copy)
            sent += 1

    def receive(item):
        remote(slot_of(item), slot_of(item), ab_s.at[0], sem_of(item), target["xM"]).wait_recv()

    def compute(color, steps):
        block, n_pairs = (block_a, PAIRS_A) if color == "A" else (block_b, PAIRS_B)
        part = NX * 2 * n_pairs
        rows = part * len(steps)
        at = [at_z(kz) for kz in steps]
        groups = NX * len(steps)

        def take(columns):
            return jnp.concatenate([block[k, :, :, columns].reshape(part, -1) for k in at], axis=0)

        made = jnp.dot(take(slice(None)), weights_t[...], preferred_element_type=F32)
        made = made.reshape(groups, 2, n_pairs, 4 * hidden)
        both = made[:, 0, :, : 2 * hidden].reshape(groups * n_pairs, 2 * hidden)
        back = made[:, 1, :, 2 * hidden :].reshape(groups * n_pairs, 2 * hidden)
        turned = pltpu.roll(both, hidden, 1)
        low = lax.broadcasted_iota(jnp.int32, both.shape, 1) < hidden
        gate = jnp.where(low, both, turned)
        up = jnp.where(low, turned, both)
        sg = jax.nn.sigmoid(gate)
        act = gate * sg
        grads = jnp.where(low, back * up * (sg * (1.0 + gate * (1.0 - sg))), back * act)
        hid = jnp.where(low, act * up, 0.0)
        grads = grads.reshape(groups, 1, n_pairs, 2 * hidden)
        hid = hid.reshape(groups, 1, n_pairs, 2 * hidden)
        nothing = jnp.zeros_like(hid)
        left = jnp.concatenate(
            [
                jnp.concatenate([grads, nothing], axis=1).reshape(rows, 2 * hidden),
                jnp.concatenate([nothing, hid], axis=1).reshape(rows, 2 * hidden),
            ],
            axis=1,
        )
        left = left.T.astype(BF16)
        wide = width // 2

        def backward(i, carry):
            columns = pl.ds(pl.multiple_of(i * wide, 128), wide)
            acc[:, columns] += jnp.dot(left, take(columns), preferred_element_type=F32)
            return carry

        lax.fori_loop(0, width // wide, backward, 0)

    quarter = width // 4
    half_w, half_m = 3 * hidden // 2, hidden

    def slice_w(ref, base):
        return lambda k: ref.at[
            pl.ds(pl.multiple_of(base + half_w * lax.rem(k, 2), 16), half_w),
            pl.ds(pl.multiple_of(quarter * lax.div(k, 2), 128), quarter),
        ]

    def slice_m(ref, base):
        return lambda k: ref.at[
            pl.ds(pl.multiple_of(base + half_m * lax.rem(k, 2), 16), half_m),
            pl.ds(pl.multiple_of(quarter * lax.div(k, 2), 128), quarter),
        ]

    pass_on(("B", 0, 0))
    pass_on(("A", 0, 0))
    waits = {}
    have = {}
    ready = {"A": [], "B": []}
    state = {"weights": False}

    def step_spread():
        waits["w1"] = exchange(slice_w(stage, 0), lambda k: spread_w.at[k], w1_s, w1_r, self_sem.at[1])
        waits["m1"] = exchange(slice_m(stage, 3 * hidden), lambda k: spread_m.at[k], m1_s, m1_r, self_sem.at[3])

    def step_gather_w():
        waits["w1"]()
        for s in range(NE):
            again_w[s, :, :] = spread_w[order[s]]
        waits["w2"] = exchange(lambda k: again_w.at[k], slice_w(weights, 0), w2_s, w2_r, self_sem.at[2])

    def step_gather_m():
        waits["m1"]()
        for s in range(NE):
            again_m[s, :, :] = spread_m[order[s]]
        waits["m2"] = exchange(lambda k: again_m.at[k], slice_m(moments, 0), m2_s, m2_r, self_sem.at[4])

    def step_weights():
        waits["w2"]()
        weights[3 * hidden : 4 * hidden, :] = weights[2 * hidden : 3 * hidden, :]
        weights_t[...] = weights[...].T
        state["weights"] = True

    step_spread()
    last = PLAN[-1][0]
    steps = [(0.25, step_gather_w), (0.36, step_gather_m), (0.5, step_weights)]
    have = {("A", 0): 1, ("B", 0): 1}
    for when, item in PLAN:
        while steps and when >= steps[0][0] * last:
            steps.pop(0)[1]()
        receive(item)
        pass_on(item)
        key = (item[0], item[2])
        have[key] = have.get(key, 0) + 1
        if have[key] == NX:
            ready[item[0]].append(item[2])
        if state["weights"]:
            for color in "AB":
                if len(ready[color]) >= 2:
                    compute(color, [ready[color].pop(0), ready[color].pop(0)])
                    break
    for color in "AB":
        while ready[color]:
            compute(color, [ready[color].pop(0), ready[color].pop(0)])
    waits["m2"]()

    gin[...] = acc[: 2 * hidden, :].astype(BF16)
    outs = [
        pltpu.make_async_copy(acc.at[pl.ds(2 * hidden, hidden)], dgrad_out, out_sem.at[0]),
        pltpu.make_async_copy(gin, gin_out, out_sem.at[1]),
        pltpu.make_async_copy(weights.at[pl.ds(2 * hidden, hidden)], wdn_out, out_sem.at[2]),
        pltpu.make_async_copy(moments.at[pl.ds(0, hidden)], mom1_out, out_sem.at[3]),
        pltpu.make_async_copy(moments.at[pl.ds(hidden, hidden)], mom2_out, out_sem.at[4]),
    ]
    for copy in outs:
        copy.start()
    for copy in pending:
        copy.wait_send()
    for copy in outs:
        copy.wait()


def local(tokens, grad_out, route_weights, expert_ids, swap_code, w_in, w_down, moment1, moment2):
    width = tokens.shape[1]
    hidden = w_down.shape[1]
    vmem, anywhere = pltpu.VMEM, pl.BlockSpec(memory_space=pl.ANY)
    half_w, half_m, quarter = 3 * hidden // 2, hidden, width // 4
    dma = pltpu.SemaphoreType.DMA
    gin, dgrad, wdn, mom1, mom2 = pl.pallas_call(
        kernel,
        out_shape=(
            jax.ShapeDtypeStruct((2 * hidden, width), BF16),
            jax.ShapeDtypeStruct((hidden, width), F32),
            jax.ShapeDtypeStruct((hidden, width), BF16),
            jax.ShapeDtypeStruct((hidden, width), BF16),
            jax.ShapeDtypeStruct((hidden, width), BF16),
        ),
        in_specs=[
            pl.BlockSpec(memory_space=pltpu.VMEM),
            pl.BlockSpec(memory_space=pltpu.VMEM),
            pl.BlockSpec(memory_space=pltpu.SMEM),
        ]
        + [anywhere] * 6,
        out_specs=(anywhere,) * 5,
        scratch_shapes=[
            vmem(tokens.shape, BF16),
            vmem(tokens.shape, BF16),
            vmem((2, hidden, width), F32),
            vmem((16 * NE, tokens.shape[0]), BF16),
            vmem((16 * NE, tokens.shape[0]), BF16),
            vmem((16 * NE, 1), F32),
            vmem((NE, tokens.shape[0]), F32),
            vmem((NE, 16, width), BF16),
            vmem((NE, 16, width), BF16),
            vmem((NZ, NX, ROWS_A, width), BF16),
            vmem((NZ, NX, ROWS_B, width), BF16),
            vmem((5 * hidden, width), BF16),
            vmem((NE, half_w, quarter), BF16),
            vmem((NE, half_m, quarter), BF16),
            vmem((NE, half_w, quarter), BF16),
            vmem((NE, half_m, quarter), BF16),
            vmem((4 * hidden, width), BF16),
            vmem((width, 4 * hidden), BF16),
            vmem((2 * hidden, width), BF16),
            vmem((4 * hidden, width), F32),
            vmem((2 * hidden, width), BF16),
            dma((7,)), dma((5,)), dma((5,)),
            dma((NE,)), dma((NE,)), dma((NE,)), dma((NE,)), dma((NE,)),
            dma((NE,)), dma((NE,)), dma((NE,)), dma((NE,)), dma((NE,)),
            dma((NX * NZ,)), dma((NX * NZ,)), dma((N_SENDS,)),
        ],
        compiler_params=pltpu.CompilerParams(
            collective_id=0, has_side_effects=True, vmem_limit_bytes=60 << 20
        ),
    )(expert_ids.T, route_weights.T, swap_code, tokens, grad_out, w_in, w_down, moment1, moment2)
    first_new = BETA_ONE * mom1.astype(F32) + (1.0 - BETA_ONE) * dgrad
    second_new = BETA_TWO * mom2.astype(F32) + (1.0 - BETA_TWO) * (dgrad * dgrad)
    fix_one = 1.0 - BETA_ONE**ADAM_STEP
    fix_two = 1.0 - BETA_TWO**ADAM_STEP
    step_size = first_new / fix_one / (jnp.sqrt(second_new / fix_two) + ADAM_EPS)
    down_new = (wdn.astype(F32) - ADAM_RATE * step_size).astype(BF16)
    return down_new[None], first_new[None], second_new[None], gin.reshape(1, 2, hidden, width)


def solution(mesh):
    rows = P(("expert", "dp"), None)
    wide = P("expert", None, "dp", None)
    slot = P("expert", "dp", None)
    return jax.shard_map(
        local,
        mesh=mesh,
        in_specs=(rows, rows, rows, rows, P(), wide, slot, slot, slot),
        out_specs=(slot, slot, slot, wide),
        check_vma=False,
    )
```

```python
import functools
import heapq

import jax
import jax.numpy as jnp
from jax import lax
from jax.experimental import pallas as pl
from jax.experimental.pallas import tpu as pltpu
from jax.sharding import PartitionSpec as P

CAP = 5
ADAM_RATE = 0.01
BETA_ONE = 0.9
BETA_TWO = 0.999
ADAM_STEP = 100.0
ADAM_EPS = 1e-08
NX, NZ = 4, 8
NE = 8
ROWS_A, ROWS_B = 32, 48
PAIRS_A, PAIRS_B = ROWS_A // 2, ROWS_B // 2
F32, BF16 = jnp.float32, jnp.bfloat16
STREAMS = {"x": (1, 0), "zM": (0, 1), "zm": (0, -1), "c": (0, 0)}


def forwards(item):
    color, kx, kz = item
    ring_z = (["zM"] if 0 <= kz < NZ // 2 else []) + (["zm"] if 1 - NZ // 2 < kz <= 0 else [])
    if color == "B":
        return ring_z + ["x", "c"] if kx == 0 else ["c"]
    return (["x"] if kx == 0 else []) + ring_z + ["c"] if kz == 0 else ring_z + ["c"]


def plan():
    free = {"x": 0.0, "z": 0.0, "c": 0.0}
    cost = {"x": 2.0, "z": 1.0, "c": 0.5}
    queue, log, number = [], [], 0

    def send(now, item):
        nonlocal number
        for stream in forwards(item):
            link = stream[0]
            free[link] = max(free[link], now) + cost[link] * (ROWS_A if item[0] == "A" else ROWS_B)
            dx, dz = STREAMS[stream]
            number += 1
            there = (item[0], item[1] + dx, item[2] + dz, int(stream == "c"))
            heapq.heappush(queue, (free[link] + 14, number, there))

    send(0, ("B", 0, 0))
    send(0, ("A", 0, 0))
    while queue:
        now, _, item = heapq.heappop(queue)
        log.append((now, item))
        if not item[3]:
            send(now, item[:3])
    return log


PLAN = plan()
N_SENDS = len(PLAN)


def kernel(
    ids_ref, route_ref, swap_ref, tok_hbm, grad_hbm, win_hbm, wdn_hbm, mom1_hbm, mom2_hbm,
    gin_out, dgrad_out, wdn_out, mom1_out, mom2_out,
    tok, gout, mom, sel_t, sel_g, scale, hits, send, recv, block_a, block_b,
    stage, spread_w, spread_m, again_w, again_m, weights, weights_t, moments, acc, made_here, made_there,
    load_sem, out_sem, self_sem, disp_s, disp_r, w1_s, w1_r, w2_s, w2_r, m1_s, m1_r, m2_s, m2_r, a_r, b_r, ab_s, ret_s, ret_r,
):
    width = tok.shape[1]
    hidden = 64
    me = lax.axis_index("expert")
    dp = lax.axis_index("dp")
    z, x = dp // NX, lax.rem(dp, NX)
    sign = 1 - 2 * lax.rem(me, 2)

    loads = [
        pltpu.make_async_copy(tok_hbm, tok, load_sem.at[0]),
        pltpu.make_async_copy(grad_hbm, gout, load_sem.at[1]),
        pltpu.make_async_copy(win_hbm.at[0, 0], stage.at[pl.ds(0, hidden)], load_sem.at[2]),
        pltpu.make_async_copy(win_hbm.at[0, 1], stage.at[pl.ds(hidden, hidden)], load_sem.at[3]),
        pltpu.make_async_copy(wdn_hbm.at[0], stage.at[pl.ds(2 * hidden, hidden)], load_sem.at[4]),
        pltpu.make_async_copy(mom1_hbm.at[0], mom.at[0], load_sem.at[5]),
        pltpu.make_async_copy(mom2_hbm.at[0], mom.at[1], load_sem.at[6]),
    ]
    for copy in loads:
        copy.start()

    side = x // 2
    role = lax.rem(me + side, 2)
    sibling = me + sign
    across = NX - 1 - x
    partner = x + 1 - 2 * lax.rem(x, 2)
    served = me + role * sign

    def at_z(step):
        return lax.rem(z + NZ - sign * step, NZ)

    target = {
        "x": (me, z * NX + partner),
        "zM": (me, at_z(-1) * NX + x),
        "zm": (me, at_z(1) * NX + x),
        "c": (sibling, dp),
    }
    barrier = pltpu.get_barrier_semaphore()
    everyone = [(lax.rem(me + i, NE), dp) for i in range(1, NE)]
    everyone += [(lax.rem(me + i, NE), z * NX + across) for i in range(NE)]
    everyone += [target["x"], target["zM"], target["zm"]]
    for device in everyone:
        pl.semaphore_signal(barrier, inc=1, device_id=device, device_id_type=pl.DeviceIdType.MESH)

    order = [jnp.int32(s) for s in range(NE)]
    for bit in range(3):
        taken = []
        for s in range(NE):
            partner = s ^ (1 << bit)
            code = swap_ref[min(s, partner)]
            swapped = lax.rem(lax.div(code, jnp.int32(1 << bit)), jnp.int32(2)) == 1
            taken.append(jnp.where(swapped, order[partner], order[s]))
        order = taken

    ids = ids_ref[...]
    route = route_ref[...]
    count = ids.shape[1]
    weight_rows = []
    for s in range(NE):
        match = ids == order[s]
        hits[s : s + 1, :] = jnp.max(jnp.where(match, 1.0, 0.0), axis=0, keepdims=True)
        weight_rows.append(jnp.sum(jnp.where(match, route, 0.0), axis=0, keepdims=True))
    earlier = lax.broadcasted_iota(jnp.int32, (count, count), 0) < lax.broadcasted_iota(jnp.int32, (count, count), 1)
    hit = hits[...]
    rank = jnp.dot(hit.astype(BF16), jnp.where(earlier, 1.0, 0.0).astype(BF16), preferred_element_type=F32)
    row16 = lax.broadcasted_iota(jnp.int32, (16, count), 0)
    row8 = lax.rem(row16, 8).astype(F32)
    first = row16 < 8
    for s in range(NE):
        chosen = jnp.where((rank[s : s + 1, :] == row8) & (hit[s : s + 1, :] > 0.5), 1.0, 0.0)
        sel_t[16 * s : 16 * s + 16, :] = jnp.where(first, chosen, 0.0).astype(BF16)
        sel_g[16 * s : 16 * s + 16, :] = jnp.where(first, 0.0, chosen).astype(BF16)
        scaled = jnp.sum(chosen * weight_rows[s], axis=1, keepdims=True)
        scale[16 * s : 16 * s + 16, :] = jnp.where(
            lax.broadcasted_iota(jnp.int32, (16, 1), 0) < 8, 1.0, scaled
        )
    loads[0].wait()
    loads[1].wait()
    tile = 512

    def select(i, carry):
        columns = pl.ds(pl.multiple_of(i * tile, tile), tile)
        rows = jnp.dot(sel_t[...], tok[:, columns], preferred_element_type=F32)
        rows += jnp.dot(sel_g[...], gout[:, columns], preferred_element_type=F32)
        send[:, :, columns] = (rows * scale[...]).astype(BF16).reshape(NE, 16, tile)
        return carry

    lax.fori_loop(0, width // tile, select, 0)
    pl.semaphore_wait(barrier, len(everyone))

    def remote(src, dst, send_sem, recv_sem, device):
        return pltpu.make_async_remote_copy(
            src_ref=src, dst_ref=dst, send_sem=send_sem, recv_sem=recv_sem,
            device_id=device, device_id_type=pl.DeviceIdType.MESH,
        )

    pending, pending_far = [], []

    def exchange(src_of, dst_of, send_sems, recv_sems, own_sem):
        copies = []
        for i in range(1, NE):
            k = lax.rem(me + i, NE)
            copy = remote(src_of(k), dst_of(me), send_sems.at[i], recv_sems.at[i], (k, dp))
            copy.start()
            copies.append(copy)
        own = pltpu.make_async_copy(src_of(me), dst_of(me), own_sem)
        own.start()
        pending.extend(copies)

        def wait():
            own.wait()
            for i in range(1, NE):
                k = lax.rem(me + NE - i, NE)
                remote(src_of(k), dst_of(k), send_sems.at[i], recv_sems.at[i], (k, dp)).wait_recv()

        return wait

    def host(src_of, dst_of, send_sems, recv_sems):
        for i in range(1, NE):
            s = lax.rem(me + i, NE)
            far = lax.rem(s + side, 2)
            device = (s + far * (1 - 2 * lax.rem(s, 2)), z * NX + x + far * (across - x))
            copy = remote(src_of(s), dst_of(me), send_sems.at[i], recv_sems.at[i], device)
            copy.start()
            pending.append(copy)

        @pl.when(role == 0)
        def _():
            pltpu.make_async_copy(src_of(me), dst_of(me), recv_sems.at[0]).start()

        copy = remote(src_of(me), dst_of(me), send_sems.at[0], recv_sems.at[0], (sibling, z * NX + across))

        @pl.when(role == 1)
        def _():
            copy.start()

        pending_far.append(copy)

        def wait():
            for i in range(NE):
                k = lax.rem(served + NE - i, NE)
                remote(dst_of(k), dst_of(k), send_sems.at[i], recv_sems.at[i], (sibling, dp)).wait_recv()

        return wait

    wait_dispatch = host(lambda k: send.at[k], lambda k: recv.at[k], disp_s, disp_r)
    for copy in loads[2:]:
        copy.wait()
    stage[3 * hidden : 4 * hidden, :] = mom[0].astype(BF16)
    stage[4 * hidden : 5 * hidden, :] = mom[1].astype(BF16)
    acc[...] = jnp.zeros_like(acc)
    wait_dispatch()

    lanes = lax.broadcasted_iota(jnp.int32, (ROWS_A + ROWS_B, NE * 16), 1)
    lines = lax.broadcasted_iota(jnp.int32, (ROWS_A + ROWS_B, NE * 16), 0)
    in_b = lines >= ROWS_A
    local_line = jnp.where(in_b, lines - ROWS_A, lines)
    pairs = jnp.where(in_b, PAIRS_B, PAIRS_A)
    is_grad = local_line >= pairs
    pair = jnp.where(is_grad, local_line - pairs, local_line) + jnp.where(in_b, PAIRS_A, 0)
    wanted = lax.div(pair, CAP) * 16 + lax.rem(pair, CAP) + jnp.where(is_grad, 8, 0)
    compact = jnp.where(lanes == wanted, 1.0, 0.0).astype(BF16)

    half = lax.rem(x, 2)

    def pack(i, carry):
        columns = pl.ds(pl.multiple_of(i * tile, tile), tile)
        rows = jnp.dot(compact, recv[:, :, columns].reshape(NE * 16, tile), preferred_element_type=F32)
        rows = rows.astype(BF16)
        block_a[0, z, half, :, columns] = rows[:ROWS_A]
        block_b[0, z, half, :, columns] = rows[ROWS_A:]
        return carry

    lax.fori_loop(0, width // tile, pack, 0)

    sent = 0

    def sem_of(item, from_sibling):
        color, kx, kz = item
        return (a_r if color == "A" else b_r).at[from_sibling, (kz + NZ // 2 - 1) * 2 + kx]

    def place(kz, from_sibling):
        return at_z(-kz if from_sibling else kz)

    def slot_of(item, from_sibling, bank):
        color, kx, kz = item
        column = half if kx == 0 else 1 - half
        return (block_a if color == "A" else block_b).at[bank, place(kz, from_sibling), column]

    def pass_on(item):
        nonlocal sent
        for stream in forwards(item):
            dx, dz = STREAMS[stream]
            there = (item[0], item[1] + dx, item[2] + dz)
            bank = int(stream == "c")
            copy = remote(
                slot_of(item, 0, 0), slot_of(item, 0, bank), ab_s.at[sent], sem_of(there, bank), target[stream]
            )
            copy.start()
            pending.append(copy)
            sent += 1

    def receive(item, from_sibling):
        slot = slot_of(item, from_sibling, from_sibling)
        remote(slot, slot, ab_s.at[0], sem_of(item, from_sibling), target["x"]).wait_recv()

    def compute(color, units):
        block, n_pairs = (block_a, PAIRS_A) if color == "A" else (block_b, PAIRS_B)
        part = 4 * n_pairs
        rows = part * len(units)
        at = [(bank, place(kz, bank)) for bank, kz in units]
        groups = 2 * len(units)

        def take(columns):
            return jnp.concatenate([block[bank, k, :, :, columns].reshape(part, -1) for bank, k in at], axis=0)

        made = jnp.dot(take(slice(None)), weights_t[...], preferred_element_type=F32)
        made = made.reshape(groups, 2, n_pairs, 4 * hidden)
        both = made[:, 0, :, : 2 * hidden].reshape(groups * n_pairs, 2 * hidden)
        back = made[:, 1, :, 2 * hidden :].reshape(groups * n_pairs, 2 * hidden)
        turned = pltpu.roll(both, hidden, 1)
        low = lax.broadcasted_iota(jnp.int32, both.shape, 1) < hidden
        gate = jnp.where(low, both, turned)
        up = jnp.where(low, turned, both)
        sg = jax.nn.sigmoid(gate)
        act = gate * sg
        grads = jnp.where(low, back * up * (sg * (1.0 + gate * (1.0 - sg))), back * act)
        hid = jnp.where(low, act * up, 0.0)
        grads = grads.reshape(groups, 1, n_pairs, 2 * hidden)
        hid = hid.reshape(groups, 1, n_pairs, 2 * hidden)
        nothing = jnp.zeros_like(hid)
        left = jnp.concatenate(
            [
                jnp.concatenate([grads, nothing], axis=1).reshape(rows, 2 * hidden),
                jnp.concatenate([nothing, hid], axis=1).reshape(rows, 2 * hidden),
            ],
            axis=1,
        )
        left = left.T.astype(BF16)
        wide = width // 2

        def backward(i, carry):
            columns = pl.ds(pl.multiple_of(i * wide, 128), wide)
            acc[:, columns] += jnp.dot(left, take(columns), preferred_element_type=F32)
            return carry

        lax.fori_loop(0, width // wide, backward, 0)

    quarter = width // 4
    half_w = half_m = 3 * hidden // 2

    def slice_w(ref, base):
        return lambda k: ref.at[
            pl.ds(pl.multiple_of(base + half_w * lax.rem(k, 2), 16), half_w),
            pl.ds(pl.multiple_of(quarter * lax.div(k, 2), 128), quarter),
        ]

    def slice_m(ref, base):
        return lambda k: ref.at[
            pl.ds(pl.multiple_of(base + half_m * lax.rem(k, 2), 16), half_m),
            pl.ds(pl.multiple_of(quarter * lax.div(k, 2), 128), quarter),
        ]

    pass_on(("B", 0, 0))
    pass_on(("A", 0, 0))
    waits = {}
    have = {}
    ready = {"A": [], "B": []}
    state = {"weights": False}

    def step_spread():
        waits["w1"] = exchange(slice_w(stage, 0), lambda k: spread_w.at[k], w1_s, w1_r, self_sem.at[0])

    def step_gather_w():
        waits["w1"]()
        for s in range(NE):
            again_w[s, :, :] = spread_w[order[s]]
        waits["w2"] = host(lambda k: again_w.at[k], slice_w(weights, 0), w2_s, w2_r)

    def step_weights():
        waits["m1"] = exchange(slice_m(stage, 2 * hidden), lambda k: spread_m.at[k], m1_s, m1_r, self_sem.at[1])
        waits["w2"]()
        weights[3 * hidden : 4 * hidden, :] = weights[2 * hidden : 3 * hidden, :]
        weights_t[...] = weights[...].T
        state["weights"] = True

    def step_gather_m():
        waits["m1"]()
        for s in range(NE):
            again_m[s, :, :] = spread_m[order[s]]
        waits["m2"] = exchange(lambda k: again_m.at[k], slice_m(moments, 0), m2_s, m2_r, self_sem.at[2])

    step_spread()
    last = PLAN[-1][0]
    steps = [(0.28, step_gather_w), (0.5, step_weights), (0.8, step_gather_m)]
    have = {}
    for when, item in PLAN:
        while steps and when >= steps[0][0] * last:
            steps.pop(0)[1]()
        item, bank = item[:3], item[3]
        receive(item, bank)
        if not bank:
            pass_on(item)
        key = (item[0], bank, item[2])
        have[key] = have.get(key, int(item[2] == 0 and not bank)) + 1
        if have[key] == 2:
            ready[item[0]].append((bank, item[2]))
        if state["weights"]:
            for color in "AB":
                if len(ready[color]) >= 4:
                    compute(color, [ready[color].pop(0) for _ in range(4)])
                    break
    for color in "AB":
        while ready[color]:
            compute(color, [ready[color].pop(0) for _ in range(min(4, len(ready[color])))])

    back = []
    for i in range(3):
        rows = pl.ds(i * hidden, hidden)
        made_here[i * hidden : (i + 1) * hidden, :] = acc[i * hidden : (i + 1) * hidden, :].astype(BF16)
        copy = remote(made_here.at[rows], made_there.at[rows], ret_s.at[i], ret_r.at[i], (sibling, z * NX + across))
        back.append(copy)

        @pl.when(role == 1)
        def _():
            copy.start()

    waits["m2"]()
    outs = [
        pltpu.make_async_copy(moments.at[pl.ds(0, hidden)], wdn_out, out_sem.at[0]),
        pltpu.make_async_copy(moments.at[pl.ds(hidden, hidden)], mom1_out, out_sem.at[1]),
        pltpu.make_async_copy(moments.at[pl.ds(2 * hidden, hidden)], mom2_out, out_sem.at[2]),
    ]
    for copy in outs:
        copy.start()
    for copy in pending:
        copy.wait_send()

    def results(made):
        return [
            pltpu.make_async_copy(made.at[pl.ds(2 * hidden, hidden)], dgrad_out, out_sem.at[3]),
            pltpu.make_async_copy(made.at[pl.ds(0, 2 * hidden)], gin_out, out_sem.at[4]),
        ]

    @pl.when(role == 0)
    def _():
        for copy in results(made_here):
            copy.start()

    @pl.when(role == 1)
    def _():
        for copy in pending_far:
            copy.wait_send()
        for copy in back:
            copy.wait()
        for copy in results(made_there):
            copy.start()

    for copy in outs + results(made_here):
        copy.wait()


def local(tokens, grad_out, route_weights, expert_ids, swap_code, w_in, w_down, moment1, moment2):
    width = tokens.shape[1]
    hidden = w_down.shape[1]
    vmem, anywhere = pltpu.VMEM, pl.BlockSpec(memory_space=pl.ANY)
    half_w, quarter = 3 * hidden // 2, width // 4
    half_m = half_w
    dma = pltpu.SemaphoreType.DMA
    gin, dgrad, wdn, mom1, mom2 = pl.pallas_call(
        kernel,
        out_shape=(
            jax.ShapeDtypeStruct((2 * hidden, width), BF16),
            jax.ShapeDtypeStruct((hidden, width), BF16),
            jax.ShapeDtypeStruct((hidden, width), BF16),
            jax.ShapeDtypeStruct((hidden, width), BF16),
            jax.ShapeDtypeStruct((hidden, width), BF16),
        ),
        in_specs=[
            pl.BlockSpec(memory_space=pltpu.VMEM),
            pl.BlockSpec(memory_space=pltpu.VMEM),
            pl.BlockSpec(memory_space=pltpu.SMEM),
        ]
        + [anywhere] * 6,
        out_specs=(anywhere,) * 5,
        scratch_shapes=[
            vmem(tokens.shape, BF16),
            vmem(tokens.shape, BF16),
            vmem((2, hidden, width), F32),
            vmem((16 * NE, tokens.shape[0]), BF16),
            vmem((16 * NE, tokens.shape[0]), BF16),
            vmem((16 * NE, 1), F32),
            vmem((NE, tokens.shape[0]), F32),
            vmem((NE, 16, width), BF16),
            vmem((NE, 16, width), BF16),
            vmem((2, NZ, 2, ROWS_A, width), BF16),
            vmem((2, NZ, 2, ROWS_B, width), BF16),
            vmem((5 * hidden, width), BF16),
            vmem((NE, half_w, quarter), BF16),
            vmem((NE, half_m, quarter), BF16),
            vmem((NE, half_w, quarter), BF16),
            vmem((NE, half_m, quarter), BF16),
            vmem((4 * hidden, width), BF16),
            vmem((width, 4 * hidden), BF16),
            vmem((3 * hidden, width), BF16),
            vmem((4 * hidden, width), F32),
            vmem((3 * hidden, width), BF16),
            vmem((3 * hidden, width), BF16),
            dma((7,)), dma((5,)), dma((3,)),
            dma((NE,)), dma((NE,)), dma((NE,)), dma((NE,)), dma((NE,)),
            dma((NE,)), dma((NE,)), dma((NE,)), dma((NE,)), dma((NE,)),
            dma((2, 2 * NZ)), dma((2, 2 * NZ)), dma((N_SENDS,)), dma((3,)), dma((3,)),
        ],
        compiler_params=pltpu.CompilerParams(
            collective_id=0, has_side_effects=True, vmem_limit_bytes=60 << 20
        ),
    )(expert_ids.T, route_weights.T, swap_code, tokens, grad_out, w_in, w_down, moment1, moment2)
    dgrad = dgrad.astype(F32)
    first_new = BETA_ONE * mom1.astype(F32) + (1.0 - BETA_ONE) * dgrad
    second_new = BETA_TWO * mom2.astype(F32) + (1.0 - BETA_TWO) * (dgrad * dgrad)
    fix_one = 1.0 - BETA_ONE**ADAM_STEP
    fix_two = 1.0 - BETA_TWO**ADAM_STEP
    step_size = first_new / fix_one / (jnp.sqrt(second_new / fix_two) + ADAM_EPS)
    down_new = (wdn.astype(F32) - ADAM_RATE * step_size).astype(BF16)
    return down_new[None], first_new[None], second_new[None], gin.reshape(1, 2, hidden, width)


def solution(mesh):
    rows = P(("expert", "dp"), None)
    wide = P("expert", None, "dp", None)
    slot = P("expert", "dp", None)
    return jax.shard_map(
        local,
        mesh=mesh,
        in_specs=(rows, rows, rows, rows, P(), wide, slot, slot, slot),
        out_specs=(slot, slot, slot, wide),
        check_vma=False,
    )
```

```python
import functools
import heapq

import jax
import jax.numpy as jnp
from jax import lax
from jax.experimental import pallas as pl
from jax.experimental.pallas import tpu as pltpu
from jax.sharding import PartitionSpec as P

CAP = 5
ADAM_RATE = 0.01
BETA_ONE = 0.9
BETA_TWO = 0.999
ADAM_STEP = 100.0
ADAM_EPS = 1e-08
NX, NZ = 4, 8
NE = 8
ROWS_A, ROWS_B = 32, 48
PAIRS_A, PAIRS_B = ROWS_A // 2, ROWS_B // 2
F32, BF16 = jnp.float32, jnp.bfloat16
STREAMS = {"x": (1, 0), "zM": (0, 1), "zm": (0, -1), "c": (0, 0)}


def forwards(item):
    color, kx, kz = item
    ring_z = (["zM"] if 0 <= kz < NZ // 2 else []) + (["zm"] if 1 - NZ // 2 < kz <= 0 else [])
    if color == "B":
        return ring_z + ["x", "c"] if kx == 0 else ["c"]
    return (["x"] if kx == 0 else []) + ring_z + ["c"] if kz == 0 else ring_z + ["c"]


def plan():
    free = {"x": 0.0, "z": 0.0, "c": 0.0}
    cost = {"x": 1.0, "z": 0.5, "c": 0.25}
    queue, log, number = [(SECOND_HALF, 0, ("own",))], [], 0

    def send(now, item):
        nonlocal number
        for stream in forwards(item[:3]):
            link = stream[0]
            free[link] = max(free[link], now) + cost[link] * (ROWS_A if item[0] == "A" else ROWS_B)
            dx, dz = STREAMS[stream]
            number += 1
            there = (item[0], item[1] + dx, item[2] + dz, item[3], int(stream == "c"))
            heapq.heappush(queue, (free[link] + 14, number, there))

    send(0, ("B", 0, 0, 0))
    send(0, ("A", 0, 0, 0))
    while queue:
        now, _, item = heapq.heappop(queue)
        log.append((now, item))
        if item[0] == "own":
            send(now, ("B", 0, 0, 1))
            send(now, ("A", 0, 0, 1))
        elif not item[4]:
            send(now, item[:4])
    return log


SECOND_HALF = 70
PLAN = plan()
N_SENDS = len(PLAN) - 1
GROUPS = (4, 4, 4, 2, 2)
WHEN = (0.34, 0.58, 0.85)


def kernel(
    ids_ref, route_ref, swap_ref, tok_hbm, grad_hbm, win_hbm, wdn_hbm, mom1_hbm, mom2_hbm,
    gin_out, dgrad_out, wdn_out, mom1_out, mom2_out,
    tok, gout, mom, sel_t, sel_g, scale, hits, send, recv, block_a, block_b,
    stage, spread_w, spread_m, again_w, again_m, weights, weights_t, moments, acc, made_here, made_there,
    load_sem, out_sem, self_sem, disp_s, disp_r, w1_s, w1_r, w2_s, w2_r, m1_s, m1_r, m2_s, m2_r, a_r, b_r, ab_s, ret_s, ret_r,
):
    width = tok.shape[1]
    hidden = 64
    me = lax.axis_index("expert")
    dp = lax.axis_index("dp")
    z, x = dp // NX, lax.rem(dp, NX)
    sign = 1 - 2 * lax.rem(me, 2)

    loads = [
        pltpu.make_async_copy(tok_hbm, tok, load_sem.at[0]),
        pltpu.make_async_copy(grad_hbm, gout, load_sem.at[1]),
        pltpu.make_async_copy(win_hbm.at[0, 0], stage.at[pl.ds(0, hidden)], load_sem.at[2]),
        pltpu.make_async_copy(win_hbm.at[0, 1], stage.at[pl.ds(hidden, hidden)], load_sem.at[3]),
        pltpu.make_async_copy(wdn_hbm.at[0], stage.at[pl.ds(2 * hidden, hidden)], load_sem.at[4]),
        pltpu.make_async_copy(mom1_hbm.at[0], mom.at[0], load_sem.at[5]),
        pltpu.make_async_copy(mom2_hbm.at[0], mom.at[1], load_sem.at[6]),
    ]
    for copy in loads:
        copy.start()

    side = x // 2
    role = lax.rem(me + side, 2)
    sibling = me + sign
    across = NX - 1 - x
    partner = x + 1 - 2 * lax.rem(x, 2)
    served = me + role * sign

    def at_z(step):
        return lax.rem(z + NZ - sign * step, NZ)

    target = {
        "x": (me, z * NX + partner),
        "zM": (me, at_z(-1) * NX + x),
        "zm": (me, at_z(1) * NX + x),
        "c": (sibling, dp),
    }
    barrier = pltpu.get_barrier_semaphore()
    everyone = [(lax.rem(me + i, NE), dp) for i in range(1, NE)]
    everyone += [(lax.rem(me + i, NE), z * NX + across) for i in range(NE)]
    everyone += [target["x"], target["zM"], target["zm"]]
    for device in everyone:
        pl.semaphore_signal(barrier, inc=1, device_id=device, device_id_type=pl.DeviceIdType.MESH)

    order = [jnp.int32(s) for s in range(NE)]
    for bit in range(3):
        taken = []
        for s in range(NE):
            partner = s ^ (1 << bit)
            code = swap_ref[min(s, partner)]
            swapped = lax.rem(lax.div(code, jnp.int32(1 << bit)), jnp.int32(2)) == 1
            taken.append(jnp.where(swapped, order[partner], order[s]))
        order = taken

    ids = ids_ref[...]
    route = route_ref[...]
    count = ids.shape[1]
    weight_rows = []
    for s in range(NE):
        match = ids == order[s]
        hits[s : s + 1, :] = jnp.max(jnp.where(match, 1.0, 0.0), axis=0, keepdims=True)
        weight_rows.append(jnp.sum(jnp.where(match, route, 0.0), axis=0, keepdims=True))
    earlier = lax.broadcasted_iota(jnp.int32, (count, count), 0) < lax.broadcasted_iota(jnp.int32, (count, count), 1)
    hit = hits[...]
    rank = jnp.dot(hit.astype(BF16), jnp.where(earlier, 1.0, 0.0).astype(BF16), preferred_element_type=F32)
    row16 = lax.broadcasted_iota(jnp.int32, (16, count), 0)
    row8 = lax.rem(row16, 8).astype(F32)
    first = row16 < 8
    for s in range(NE):
        chosen = jnp.where((rank[s : s + 1, :] == row8) & (hit[s : s + 1, :] > 0.5), 1.0, 0.0)
        sel_t[16 * s : 16 * s + 16, :] = jnp.where(first, chosen, 0.0).astype(BF16)
        sel_g[16 * s : 16 * s + 16, :] = jnp.where(first, 0.0, chosen).astype(BF16)
        scaled = jnp.sum(chosen * weight_rows[s], axis=1, keepdims=True)
        scale[16 * s : 16 * s + 16, :] = jnp.where(
            lax.broadcasted_iota(jnp.int32, (16, 1), 0) < 8, 1.0, scaled
        )
    loads[0].wait()
    loads[1].wait()
    tile = width // 4

    def select(i, carry):
        columns = pl.ds(pl.multiple_of(i * tile, tile), tile)
        rows = jnp.dot(sel_t[...], tok[:, columns], preferred_element_type=F32)
        rows += jnp.dot(sel_g[...], gout[:, columns], preferred_element_type=F32)
        send[:, :, columns] = (rows * scale[...]).astype(BF16).reshape(NE, 16, tile)
        return carry

    lax.fori_loop(0, 2, select, 0)
    pl.semaphore_wait(barrier, len(everyone))

    def remote(src, dst, send_sem, recv_sem, device):
        return pltpu.make_async_remote_copy(
            src_ref=src, dst_ref=dst, send_sem=send_sem, recv_sem=recv_sem,
            device_id=device, device_id_type=pl.DeviceIdType.MESH,
        )

    pending, pending_far = [], []

    def exchange(src_of, dst_of, send_sems, recv_sems, own_sem):
        copies = []
        for i in range(1, NE):
            k = lax.rem(me + i, NE)
            copy = remote(src_of(k), dst_of(me), send_sems.at[i], recv_sems.at[i], (k, dp))
            copy.start()
            copies.append(copy)
        own = pltpu.make_async_copy(src_of(me), dst_of(me), own_sem)
        own.start()
        pending.extend(copies)

        def wait():
            own.wait()
            for i in range(1, NE):
                k = lax.rem(me + NE - i, NE)
                remote(src_of(k), dst_of(k), send_sems.at[i], recv_sems.at[i], (k, dp)).wait_recv()

        return wait

    def host(src_of, dst_of, send_sems, recv_sems):
        for i in range(1, NE):
            s = lax.rem(me + i, NE)
            far = lax.rem(s + side, 2)
            device = (s + far * (1 - 2 * lax.rem(s, 2)), z * NX + x + far * (across - x))
            copy = remote(src_of(s), dst_of(me), send_sems.at[i], recv_sems.at[i], device)
            copy.start()
            pending.append(copy)

        @pl.when(role == 0)
        def _():
            pltpu.make_async_copy(src_of(me), dst_of(me), recv_sems.at[0]).start()

        copy = remote(src_of(me), dst_of(me), send_sems.at[0], recv_sems.at[0], (sibling, z * NX + across))

        @pl.when(role == 1)
        def _():
            copy.start()

        pending_far.append(copy)

        def wait():
            for i in range(NE):
                k = lax.rem(served + NE - i, NE)
                remote(dst_of(k), dst_of(k), send_sems.at[i], recv_sems.at[i], (sibling, dp)).wait_recv()

        return wait

    def dispatch(part):
        columns = pl.ds(part * (width // 2), width // 2)
        return host(
            lambda k: send.at[k, :, columns], lambda k: recv.at[k, :, columns], disp_s.at[part], disp_r.at[part]
        )

    wait_first = dispatch(0)
    lax.fori_loop(2, 4, select, 0)
    wait_second = dispatch(1)
    for copy in loads[2:]:
        copy.wait()
    stage[3 * hidden : 4 * hidden, :] = mom[0].astype(BF16)
    stage[4 * hidden : 5 * hidden, :] = mom[1].astype(BF16)
    acc[...] = jnp.zeros_like(acc)
    wait_first()

    lanes = lax.broadcasted_iota(jnp.int32, (ROWS_A + ROWS_B, NE * 16), 1)
    lines = lax.broadcasted_iota(jnp.int32, (ROWS_A + ROWS_B, NE * 16), 0)
    in_b = lines >= ROWS_A
    local_line = jnp.where(in_b, lines - ROWS_A, lines)
    pairs = jnp.where(in_b, PAIRS_B, PAIRS_A)
    is_grad = local_line >= pairs
    pair = jnp.where(is_grad, local_line - pairs, local_line) + jnp.where(in_b, PAIRS_A, 0)
    wanted = lax.div(pair, CAP) * 16 + lax.rem(pair, CAP) + jnp.where(is_grad, 8, 0)
    compact = jnp.where(lanes == wanted, 1.0, 0.0).astype(BF16)

    half = lax.rem(x, 2)

    def pack(i, carry):
        columns = pl.ds(pl.multiple_of(i * tile, tile), tile)
        rows = jnp.dot(compact, recv[:, :, columns].reshape(NE * 16, tile), preferred_element_type=F32)
        rows = rows.astype(BF16)
        block_a[0, z, half, :, columns] = rows[:ROWS_A]
        block_b[0, z, half, :, columns] = rows[ROWS_A:]
        return carry

    lax.fori_loop(0, 2, pack, 0)

    sent = 0

    def sem_of(item, from_sibling):
        color, kx, kz, part = item
        return (a_r if color == "A" else b_r).at[from_sibling, part, (kz + NZ // 2 - 1) * 2 + kx]

    def place(kz, from_sibling):
        return at_z(-kz if from_sibling else kz)

    def slot_of(item, from_sibling, bank):
        color, kx, kz, part = item
        column = half if kx == 0 else 1 - half
        columns = pl.ds(part * (width // 2), width // 2)
        return (block_a if color == "A" else block_b).at[bank, place(kz, from_sibling), column, :, columns]

    def pass_on(item):
        nonlocal sent
        for stream in forwards(item[:3]):
            dx, dz = STREAMS[stream]
            there = (item[0], item[1] + dx, item[2] + dz, item[3])
            bank = int(stream == "c")
            copy = remote(
                slot_of(item, 0, 0), slot_of(item, 0, bank), ab_s.at[sent], sem_of(there, bank), target[stream]
            )
            copy.start()
            pending.append(copy)
            sent += 1

    def receive(item, from_sibling):
        slot = slot_of(item, from_sibling, from_sibling)
        remote(slot, slot, ab_s.at[0], sem_of(item, from_sibling), target["x"]).wait_recv()

    def compute(color, units):
        block, n_pairs = (block_a, PAIRS_A) if color == "A" else (block_b, PAIRS_B)
        part = 4 * n_pairs
        rows = part * len(units)
        at = [(bank, place(kz, bank)) for bank, kz in units]
        groups = 2 * len(units)

        def take(columns):
            return jnp.concatenate([block[bank, k, :, :, columns].reshape(part, -1) for bank, k in at], axis=0)

        made = jnp.dot(take(slice(None)), weights_t[...], preferred_element_type=F32)
        made = made.reshape(groups, 2, n_pairs, 4 * hidden)
        both = made[:, 0, :, : 2 * hidden].reshape(groups * n_pairs, 2 * hidden)
        back = made[:, 1, :, 2 * hidden :].reshape(groups * n_pairs, 2 * hidden)
        turned = pltpu.roll(both, hidden, 1)
        low = lax.broadcasted_iota(jnp.int32, both.shape, 1) < hidden
        gate = jnp.where(low, both, turned)
        up = jnp.where(low, turned, both)
        sg = jax.nn.sigmoid(gate)
        act = gate * sg
        grads = jnp.where(low, back * up * (sg * (1.0 + gate * (1.0 - sg))), back * act)
        hid = jnp.where(low, act * up, 0.0)
        grads = grads.reshape(groups, 1, n_pairs, 2 * hidden)
        hid = hid.reshape(groups, 1, n_pairs, 2 * hidden)
        nothing = jnp.zeros_like(hid)
        left = jnp.concatenate(
            [
                jnp.concatenate([grads, nothing], axis=1).reshape(rows, 2 * hidden),
                jnp.concatenate([nothing, hid], axis=1).reshape(rows, 2 * hidden),
            ],
            axis=1,
        )
        left = left.T.astype(BF16)
        wide = width // 2

        def backward(i, carry):
            columns = pl.ds(pl.multiple_of(i * wide, 128), wide)
            acc[:, columns] += jnp.dot(left, take(columns), preferred_element_type=F32)
            return carry

        lax.fori_loop(0, width // wide, backward, 0)

    quarter = width // 4
    half_w = half_m = 3 * hidden // 2

    def slice_w(ref, base):
        return lambda k: ref.at[
            pl.ds(pl.multiple_of(base + half_w * lax.rem(k, 2), 16), half_w),
            pl.ds(pl.multiple_of(quarter * lax.div(k, 2), 128), quarter),
        ]

    def slice_m(ref, base):
        return lambda k: ref.at[
            pl.ds(pl.multiple_of(base + half_m * lax.rem(k, 2), 16), half_m),
            pl.ds(pl.multiple_of(quarter * lax.div(k, 2), 128), quarter),
        ]

    pass_on(("B", 0, 0, 0))
    pass_on(("A", 0, 0, 0))
    waits = {}
    have = {}
    ready = {"A": [], "B": []}
    state = {"weights": False}

    def step_spread():
        waits["w1"] = exchange(slice_w(stage, 0), lambda k: spread_w.at[k], w1_s, w1_r, self_sem.at[0])

    def step_gather_w():
        waits["w1"]()
        for s in range(NE):
            again_w[s, :, :] = spread_w[order[s]]
        waits["w2"] = host(lambda k: again_w.at[k], slice_w(weights, 0), w2_s, w2_r)

    def step_weights():
        waits["m1"] = exchange(slice_m(stage, 2 * hidden), lambda k: spread_m.at[k], m1_s, m1_r, self_sem.at[1])
        waits["w2"]()
        weights[3 * hidden : 4 * hidden, :] = weights[2 * hidden : 3 * hidden, :]
        weights_t[...] = weights[...].T
        state["weights"] = True

    def step_gather_m():
        waits["m1"]()
        for s in range(NE):
            again_m[s, :, :] = spread_m[order[s]]
        waits["m2"] = exchange(lambda k: again_m.at[k], slice_m(moments, 0), m2_s, m2_r, self_sem.at[2])

    last = PLAN[-1][0]
    steps = list(zip(WHEN, (step_gather_w, step_weights, step_gather_m)))
    have = {}
    sizes = {"A": list(GROUPS), "B": list(GROUPS)}
    for when, item in PLAN:
        while steps and when >= steps[0][0] * last:
            steps.pop(0)[1]()
        if item[0] == "own":
            wait_second()
            lax.fori_loop(2, 4, pack, 0)
            pass_on(("B", 0, 0, 1))
            pass_on(("A", 0, 0, 1))
            step_spread()
            continue
        item, bank = item[:4], item[4]
        receive(item, bank)
        if not bank:
            pass_on(item)
        key = (item[0], bank, item[2])
        have[key] = have.get(key, 2 * int(item[2] == 0 and not bank)) + 1
        if have[key] == 4:
            ready[item[0]].append((bank, item[2]))
        if state["weights"]:
            for color in "AB":
                if sizes[color] and len(ready[color]) >= sizes[color][0]:
                    compute(color, [ready[color].pop(0) for _ in range(sizes[color].pop(0))])
                    break
    for color in "AB":
        for size in sizes[color]:
            compute(color, [ready[color].pop(0) for _ in range(size)])

    back = []
    for i in range(3):
        rows = pl.ds(i * hidden, hidden)
        made_here[i * hidden : (i + 1) * hidden, :] = acc[i * hidden : (i + 1) * hidden, :].astype(BF16)
        copy = remote(made_here.at[rows], made_there.at[rows], ret_s.at[i], ret_r.at[i], (sibling, z * NX + across))
        back.append(copy)

        @pl.when(role == 1)
        def _():
            copy.start()

    waits["m2"]()
    outs = [
        pltpu.make_async_copy(moments.at[pl.ds(0, hidden)], wdn_out, out_sem.at[0]),
        pltpu.make_async_copy(moments.at[pl.ds(hidden, hidden)], mom1_out, out_sem.at[1]),
        pltpu.make_async_copy(moments.at[pl.ds(2 * hidden, hidden)], mom2_out, out_sem.at[2]),
    ]
    for copy in outs:
        copy.start()
    for copy in pending:
        copy.wait_send()

    def results(made):
        return [
            pltpu.make_async_copy(made.at[pl.ds(2 * hidden, hidden)], dgrad_out, out_sem.at[3]),
            pltpu.make_async_copy(made.at[pl.ds(0, 2 * hidden)], gin_out, out_sem.at[4]),
        ]

    @pl.when(role == 0)
    def _():
        for copy in results(made_here):
            copy.start()

    @pl.when(role == 1)
    def _():
        for copy in pending_far:
            copy.wait_send()
        for copy in back:
            copy.wait()
        for copy in results(made_there):
            copy.start()

    for copy in outs + results(made_here):
        copy.wait()


def local(tokens, grad_out, route_weights, expert_ids, swap_code, w_in, w_down, moment1, moment2):
    width = tokens.shape[1]
    hidden = w_down.shape[1]
    vmem, anywhere = pltpu.VMEM, pl.BlockSpec(memory_space=pl.ANY)
    half_w, quarter = 3 * hidden // 2, width // 4
    half_m = half_w
    dma = pltpu.SemaphoreType.DMA
    gin, dgrad, wdn, mom1, mom2 = pl.pallas_call(
        kernel,
        out_shape=(
            jax.ShapeDtypeStruct((2 * hidden, width), BF16),
            jax.ShapeDtypeStruct((hidden, width), BF16),
            jax.ShapeDtypeStruct((hidden, width), BF16),
            jax.ShapeDtypeStruct((hidden, width), BF16),
            jax.ShapeDtypeStruct((hidden, width), BF16),
        ),
        in_specs=[
            pl.BlockSpec(memory_space=pltpu.VMEM),
            pl.BlockSpec(memory_space=pltpu.VMEM),
            pl.BlockSpec(memory_space=pltpu.SMEM),
        ]
        + [anywhere] * 6,
        out_specs=(anywhere,) * 5,
        scratch_shapes=[
            vmem(tokens.shape, BF16),
            vmem(tokens.shape, BF16),
            vmem((2, hidden, width), F32),
            vmem((16 * NE, tokens.shape[0]), BF16),
            vmem((16 * NE, tokens.shape[0]), BF16),
            vmem((16 * NE, 1), F32),
            vmem((NE, tokens.shape[0]), F32),
            vmem((NE, 16, width), BF16),
            vmem((NE, 16, width), BF16),
            vmem((2, NZ, 2, ROWS_A, width), BF16),
            vmem((2, NZ, 2, ROWS_B, width), BF16),
            vmem((5 * hidden, width), BF16),
            vmem((NE, half_w, quarter), BF16),
            vmem((NE, half_m, quarter), BF16),
            vmem((NE, half_w, quarter), BF16),
            vmem((NE, half_m, quarter), BF16),
            vmem((4 * hidden, width), BF16),
            vmem((width, 4 * hidden), BF16),
            vmem((3 * hidden, width), BF16),
            vmem((4 * hidden, width), F32),
            vmem((3 * hidden, width), BF16),
            vmem((3 * hidden, width), BF16),
            dma((7,)), dma((5,)), dma((3,)),
            dma((2, NE)), dma((2, NE)), dma((NE,)), dma((NE,)), dma((NE,)),
            dma((NE,)), dma((NE,)), dma((NE,)), dma((NE,)), dma((NE,)),
            dma((2, 2, 2 * NZ)), dma((2, 2, 2 * NZ)), dma((N_SENDS,)), dma((3,)), dma((3,)),
        ],
        compiler_params=pltpu.CompilerParams(
            collective_id=0, has_side_effects=True, vmem_limit_bytes=60 << 20
        ),
    )(expert_ids.T, route_weights.T, swap_code, tokens, grad_out, w_in, w_down, moment1, moment2)
    steps = 2
    thin = pl.BlockSpec((hidden // steps, width), lambda i: (i, 0))
    thick = pl.BlockSpec((2 * hidden // steps, width), lambda i: (i, 0))
    down_new, first_new, second_new, in_new = pl.pallas_call(
        adam,
        grid=(steps,),
        out_shape=(
            jax.ShapeDtypeStruct((hidden, width), BF16),
            jax.ShapeDtypeStruct((hidden, width), F32),
            jax.ShapeDtypeStruct((hidden, width), F32),
            jax.ShapeDtypeStruct((2 * hidden, width), BF16),
        ),
        in_specs=[thick, thin, thin, thin, thin],
        out_specs=(thin, thin, thin, thick),
        compiler_params=pltpu.CompilerParams(vmem_limit_bytes=60 << 20),
    )(gin, dgrad, wdn, mom1, mom2)
    return down_new[None], first_new[None], second_new[None], in_new.reshape(1, 2, hidden, width)


def adam(gin, dgrad, wdn, mom1, mom2, down_new, first_new, second_new, in_new):
    grad = dgrad[...].astype(F32)
    first = BETA_ONE * mom1[...].astype(F32) + (1.0 - BETA_ONE) * grad
    second = BETA_TWO * mom2[...].astype(F32) + (1.0 - BETA_TWO) * (grad * grad)
    fix_one = 1.0 - BETA_ONE**ADAM_STEP
    fix_two = 1.0 - BETA_TWO**ADAM_STEP
    step_size = first * (1.0 / fix_one) / (jnp.sqrt(second * (1.0 / fix_two)) + ADAM_EPS)
    down_new[...] = (wdn[...].astype(F32) - ADAM_RATE * step_size).astype(BF16)
    first_new[...] = first
    second_new[...] = second
    in_new[...] = gin[...]


def solution(mesh):
    rows = P(("expert", "dp"), None)
    wide = P("expert", None, "dp", None)
    slot = P("expert", "dp", None)
    return jax.shard_map(
        local,
        mesh=mesh,
        in_specs=(rows, rows, rows, rows, P(), wide, slot, slot, slot),
        out_specs=(slot, slot, slot, wide),
        check_vma=False,
    )
```

```python
import functools
import heapq

import jax
import jax.numpy as jnp
from jax import lax
from jax.experimental import pallas as pl
from jax.experimental.pallas import tpu as pltpu
from jax.sharding import PartitionSpec as P

CAP = 5
ADAM_RATE = 0.01
BETA_ONE = 0.9
BETA_TWO = 0.999
ADAM_STEP = 100.0
ADAM_EPS = 1e-08
NX, NZ = 4, 8
NE = 8
ROWS_A, ROWS_B = 32, 48
PAIRS_A, PAIRS_B = ROWS_A // 2, ROWS_B // 2
F32, BF16 = jnp.float32, jnp.bfloat16
STREAMS = {"x": (1, 0), "zM": (0, 1), "zm": (0, -1), "c": (0, 0)}


def forwards(item):
    color, kx, kz = item
    ring_z = (["zM"] if 0 <= kz < NZ // 2 else []) + (["zm"] if 1 - NZ // 2 < kz <= 0 else [])
    if color == "B":
        return ring_z + ["x", "c"] if kx == 0 else ["c"]
    return (["x"] if kx == 0 else []) + ring_z + ["c"] if kz == 0 else ring_z + ["c"]


def plan():
    free = {"x": 0.0, "z": 0.0, "c": 0.0}
    cost = {"x": 1.0, "z": 0.5, "c": 0.25}
    queue, log, number = [(SECOND_HALF, 0, ("own",))], [], 0

    def send(now, item):
        nonlocal number
        for stream in forwards(item[:3]):
            link = stream[0]
            free[link] = max(free[link], now) + cost[link] * (ROWS_A if item[0] == "A" else ROWS_B)
            dx, dz = STREAMS[stream]
            number += 1
            there = (item[0], item[1] + dx, item[2] + dz, item[3], int(stream == "c"))
            heapq.heappush(queue, (free[link] + 14, number, there))

    send(0, ("B", 0, 0, 0))
    send(0, ("A", 0, 0, 0))
    while queue:
        now, _, item = heapq.heappop(queue)
        log.append((now, item))
        if item[0] == "own":
            send(now, ("B", 0, 0, 1))
            send(now, ("A", 0, 0, 1))
        elif not item[4]:
            send(now, item[:4])
    return log


SECOND_HALF = 70
PLAN = plan()
N_SENDS = len(PLAN) - 1
GROUPS = (4, 4, 4, 2, 2)
WHEN = (0.34, 0.58, 0.85)


def kernel(
    ids_ref, route_ref, swap_ref, tok_hbm, grad_hbm, win_hbm, wdn_hbm, mom1_hbm, mom2_hbm,
    gin_out, dgrad_out, wdn_out, mom1_out, mom2_out,
    tok, gout, mom, sel_t, sel_g, scale, hits, send, recv, block_a, block_b,
    stage, spread_w, spread_m, again_w, again_m, weights, weights_t, moments, acc, made_here, made_there,
    load_sem, out_sem, self_sem, disp_s, disp_r, w1_s, w1_r, w2_s, w2_r, m1_s, m1_r, m2_s, m2_r, a_r, b_r, ab_s, ret_s, ret_r,
):
    width = tok.shape[1]
    hidden = 64
    me = lax.axis_index("expert")
    dp = lax.axis_index("dp")
    z, x = dp // NX, lax.rem(dp, NX)
    sign = 1 - 2 * lax.rem(me, 2)

    loads = [
        pltpu.make_async_copy(tok_hbm, tok, load_sem.at[0]),
        pltpu.make_async_copy(grad_hbm, gout, load_sem.at[1]),
        pltpu.make_async_copy(win_hbm.at[0, 0], stage.at[pl.ds(0, hidden)], load_sem.at[2]),
        pltpu.make_async_copy(win_hbm.at[0, 1], stage.at[pl.ds(hidden, hidden)], load_sem.at[3]),
        pltpu.make_async_copy(wdn_hbm.at[0], stage.at[pl.ds(2 * hidden, hidden)], load_sem.at[4]),
        pltpu.make_async_copy(mom1_hbm.at[0], mom.at[0], load_sem.at[5]),
        pltpu.make_async_copy(mom2_hbm.at[0], mom.at[1], load_sem.at[6]),
    ]
    for copy in loads:
        copy.start()

    side = x // 2
    role = lax.rem(me + side, 2)
    sibling = me + sign
    across = NX - 1 - x
    partner = x + 1 - 2 * lax.rem(x, 2)
    served = me + role * sign

    def at_z(step):
        return lax.rem(z + NZ - sign * step, NZ)

    target = {
        "x": (me, z * NX + partner),
        "zM": (me, at_z(-1) * NX + x),
        "zm": (me, at_z(1) * NX + x),
        "c": (sibling, dp),
    }
    barrier = pltpu.get_barrier_semaphore()
    everyone = [(lax.rem(me + i, NE), dp) for i in range(1, NE)]
    everyone += [(lax.rem(me + i, NE), z * NX + across) for i in range(NE)]
    everyone += [target["x"], target["zM"], target["zm"]]
    for device in everyone:
        pl.semaphore_signal(barrier, inc=1, device_id=device, device_id_type=pl.DeviceIdType.MESH)

    order = [jnp.int32(s) for s in range(NE)]
    for bit in range(3):
        taken = []
        for s in range(NE):
            partner = s ^ (1 << bit)
            code = swap_ref[min(s, partner)]
            swapped = lax.rem(lax.div(code, jnp.int32(1 << bit)), jnp.int32(2)) == 1
            taken.append(jnp.where(swapped, order[partner], order[s]))
        order = taken

    ids = ids_ref[...]
    route = route_ref[...]
    count = ids.shape[1]
    weight_rows = []
    for s in range(NE):
        match = ids == order[s]
        hits[s : s + 1, :] = jnp.max(jnp.where(match, 1.0, 0.0), axis=0, keepdims=True)
        weight_rows.append(jnp.sum(jnp.where(match, route, 0.0), axis=0, keepdims=True))
    earlier = lax.broadcasted_iota(jnp.int32, (count, count), 0) < lax.broadcasted_iota(jnp.int32, (count, count), 1)
    hit = hits[...]
    rank = jnp.dot(hit.astype(BF16), jnp.where(earlier, 1.0, 0.0).astype(BF16), preferred_element_type=F32)
    row16 = lax.broadcasted_iota(jnp.int32, (16, count), 0)
    row8 = lax.rem(row16, 8).astype(F32)
    first = row16 < 8
    for s in range(NE):
        chosen = jnp.where((rank[s : s + 1, :] == row8) & (hit[s : s + 1, :] > 0.5), 1.0, 0.0)
        sel_t[16 * s : 16 * s + 16, :] = jnp.where(first, chosen, 0.0).astype(BF16)
        sel_g[16 * s : 16 * s + 16, :] = jnp.where(first, 0.0, chosen).astype(BF16)
        scaled = jnp.sum(chosen * weight_rows[s], axis=1, keepdims=True)
        scale[16 * s : 16 * s + 16, :] = jnp.where(
            lax.broadcasted_iota(jnp.int32, (16, 1), 0) < 8, 1.0, scaled
        )
    loads[0].wait()
    loads[1].wait()
    tile = width // 4

    def select(i, carry):
        columns = pl.ds(pl.multiple_of(i * tile, tile), tile)
        rows = jnp.dot(sel_t[...], tok[:, columns], preferred_element_type=F32)
        rows += jnp.dot(sel_g[...], gout[:, columns], preferred_element_type=F32)
        send[:, :, columns] = (rows * scale[...]).astype(BF16).reshape(NE, 16, tile)
        return carry

    lax.fori_loop(0, 2, select, 0)
    pl.semaphore_wait(barrier, len(everyone))

    def remote(src, dst, send_sem, recv_sem, device):
        return pltpu.make_async_remote_copy(
            src_ref=src, dst_ref=dst, send_sem=send_sem, recv_sem=recv_sem,
            device_id=device, device_id_type=pl.DeviceIdType.MESH,
        )

    pending, pending_far = [], []

    def exchange(src_of, dst_of, send_sems, recv_sems, own_sem):
        copies = []
        for i in range(1, NE):
            k = lax.rem(me + i, NE)
            copy = remote(src_of(k), dst_of(me), send_sems.at[i], recv_sems.at[i], (k, dp))
            copy.start()
            copies.append(copy)
        own = pltpu.make_async_copy(src_of(me), dst_of(me), own_sem)
        own.start()
        pending.extend(copies)

        def wait():
            own.wait()
            for i in range(1, NE):
                k = lax.rem(me + NE - i, NE)
                remote(src_of(k), dst_of(k), send_sems.at[i], recv_sems.at[i], (k, dp)).wait_recv()

        return wait

    def host(src_of, dst_of, send_sems, recv_sems):
        for i in range(1, NE):
            s = lax.rem(me + i, NE)
            far = lax.rem(s + side, 2)
            device = (s + far * (1 - 2 * lax.rem(s, 2)), z * NX + x + far * (across - x))
            copy = remote(src_of(s), dst_of(me), send_sems.at[i], recv_sems.at[i], device)
            copy.start()
            pending.append(copy)

        @pl.when(role == 0)
        def _():
            pltpu.make_async_copy(src_of(me), dst_of(me), recv_sems.at[0]).start()

        copy = remote(src_of(me), dst_of(me), send_sems.at[0], recv_sems.at[0], (sibling, z * NX + across))

        @pl.when(role == 1)
        def _():
            copy.start()

        pending_far.append(copy)

        def wait():
            for i in range(NE):
                k = lax.rem(served + NE - i, NE)
                remote(dst_of(k), dst_of(k), send_sems.at[i], recv_sems.at[i], (sibling, dp)).wait_recv()

        return wait

    def dispatch(part):
        columns = pl.ds(part * (width // 2), width // 2)
        return host(
            lambda k: send.at[k, :, columns], lambda k: recv.at[k, :, columns], disp_s.at[part], disp_r.at[part]
        )

    wait_first = dispatch(0)
    lax.fori_loop(2, 4, select, 0)
    wait_second = dispatch(1)
    for copy in loads[2:]:
        copy.wait()
    stage[3 * hidden : 4 * hidden, :] = mom[0].astype(BF16)
    stage[4 * hidden : 5 * hidden, :] = mom[1].astype(BF16)
    acc[...] = jnp.zeros_like(acc)
    wait_first()

    lanes = lax.broadcasted_iota(jnp.int32, (ROWS_A + ROWS_B, NE * 16), 1)
    lines = lax.broadcasted_iota(jnp.int32, (ROWS_A + ROWS_B, NE * 16), 0)
    in_b = lines >= ROWS_A
    local_line = jnp.where(in_b, lines - ROWS_A, lines)
    pairs = jnp.where(in_b, PAIRS_B, PAIRS_A)
    is_grad = local_line >= pairs
    pair = jnp.where(is_grad, local_line - pairs, local_line) + jnp.where(in_b, PAIRS_A, 0)
    wanted = lax.div(pair, CAP) * 16 + lax.rem(pair, CAP) + jnp.where(is_grad, 8, 0)
    compact = jnp.where(lanes == wanted, 1.0, 0.0).astype(BF16)

    half = lax.rem(x, 2)

    def pack(i, carry):
        columns = pl.ds(pl.multiple_of(i * tile, tile), tile)
        rows = jnp.dot(compact, recv[:, :, columns].reshape(NE * 16, tile), preferred_element_type=F32)
        rows = rows.astype(BF16)
        block_a[0, z, half, :, columns] = rows[:ROWS_A]
        block_b[0, z, half, :, columns] = rows[ROWS_A:]
        return carry

    lax.fori_loop(0, 2, pack, 0)

    sent = 0

    def sem_of(item, from_sibling):
        color, kx, kz, part = item
        return (a_r if color == "A" else b_r).at[from_sibling, part, (kz + NZ // 2 - 1) * 2 + kx]

    def place(kz, from_sibling):
        return at_z(-kz if from_sibling else kz)

    def slot_of(item, from_sibling, bank):
        color, kx, kz, part = item
        column = half if kx == 0 else 1 - half
        columns = pl.ds(part * (width // 2), width // 2)
        return (block_a if color == "A" else block_b).at[bank, place(kz, from_sibling), column, :, columns]

    def pass_on(item):
        nonlocal sent
        for stream in forwards(item[:3]):
            dx, dz = STREAMS[stream]
            there = (item[0], item[1] + dx, item[2] + dz, item[3])
            bank = int(stream == "c")
            copy = remote(
                slot_of(item, 0, 0), slot_of(item, 0, bank), ab_s.at[sent], sem_of(there, bank), target[stream]
            )
            copy.start()
            pending.append(copy)
            sent += 1

    def receive(item, from_sibling):
        slot = slot_of(item, from_sibling, from_sibling)
        remote(slot, slot, ab_s.at[0], sem_of(item, from_sibling), target["x"]).wait_recv()

    def compute(color, units):
        block, n_pairs = (block_a, PAIRS_A) if color == "A" else (block_b, PAIRS_B)
        part = 4 * n_pairs
        rows = part * len(units)
        at = [(bank, place(kz, bank)) for bank, kz in units]
        groups = 2 * len(units)

        def take(columns):
            return jnp.concatenate([block[bank, k, :, :, columns].reshape(part, -1) for bank, k in at], axis=0)

        made = jnp.dot(take(slice(None)), weights_t[...], preferred_element_type=F32)
        made = made.reshape(groups, 2, n_pairs, 4 * hidden)
        both = made[:, 0, :, : 2 * hidden].reshape(groups * n_pairs, 2 * hidden)
        back = made[:, 1, :, 2 * hidden :].reshape(groups * n_pairs, 2 * hidden)
        turned = pltpu.roll(both, hidden, 1)
        low = lax.broadcasted_iota(jnp.int32, both.shape, 1) < hidden
        gate = jnp.where(low, both, turned)
        up = jnp.where(low, turned, both)
        sg = jax.nn.sigmoid(gate)
        act = gate * sg
        grads = jnp.where(low, back * up * (sg * (1.0 + gate * (1.0 - sg))), back * act)
        hid = jnp.where(low, act * up, 0.0)
        grads = grads.reshape(groups, 1, n_pairs, 2 * hidden)
        hid = hid.reshape(groups, 1, n_pairs, 2 * hidden)
        nothing = jnp.zeros_like(hid)
        left = jnp.concatenate(
            [
                jnp.concatenate([grads, nothing], axis=1).reshape(rows, 2 * hidden),
                jnp.concatenate([nothing, hid], axis=1).reshape(rows, 2 * hidden),
            ],
            axis=1,
        )
        left = left.T.astype(BF16)
        wide = width // 2

        def backward(i, carry):
            columns = pl.ds(pl.multiple_of(i * wide, 128), wide)
            acc[:, columns] += jnp.dot(left, take(columns), preferred_element_type=F32)
            return carry

        lax.fori_loop(0, width // wide, backward, 0)

    quarter = width // 4
    half_w = half_m = 3 * hidden // 2

    def slice_w(ref, base):
        return lambda k: ref.at[
            pl.ds(pl.multiple_of(base + half_w * lax.rem(k, 2), 16), half_w),
            pl.ds(pl.multiple_of(quarter * lax.div(k, 2), 128), quarter),
        ]

    def slice_m(ref, base):
        return lambda k: ref.at[
            pl.ds(pl.multiple_of(base + half_m * lax.rem(k, 2), 16), half_m),
            pl.ds(pl.multiple_of(quarter * lax.div(k, 2), 128), quarter),
        ]

    pass_on(("B", 0, 0, 0))
    pass_on(("A", 0, 0, 0))
    waits = {}
    have = {}
    ready = {"A": [], "B": []}
    state = {"weights": False}

    def step_spread():
        waits["w1"] = exchange(slice_w(stage, 0), lambda k: spread_w.at[k], w1_s, w1_r, self_sem.at[0])

    def step_gather_w():
        waits["w1"]()
        for s in range(NE):
            again_w[s, :, :] = spread_w[order[s]]
        waits["w2"] = host(lambda k: again_w.at[k], slice_w(weights, 0), w2_s, w2_r)

    def step_weights():
        waits["m1"] = exchange(slice_m(stage, 2 * hidden), lambda k: spread_m.at[k], m1_s, m1_r, self_sem.at[1])
        waits["w2"]()
        weights[3 * hidden : 4 * hidden, :] = weights[2 * hidden : 3 * hidden, :]
        weights_t[...] = weights[...].T
        state["weights"] = True

    def step_gather_m():
        waits["m1"]()
        for s in range(NE):
            again_m[s, :, :] = spread_m[order[s]]
        waits["m2"] = exchange(lambda k: again_m.at[k], slice_m(moments, 0), m2_s, m2_r, self_sem.at[2])

    last = PLAN[-1][0]
    steps = list(zip(WHEN, (step_gather_w, step_weights, step_gather_m)))
    have = {}
    sizes = {"A": list(GROUPS), "B": list(GROUPS)}
    for when, item in PLAN:
        while steps and when >= steps[0][0] * last:
            steps.pop(0)[1]()
        if item[0] == "own":
            wait_second()
            lax.fori_loop(2, 4, pack, 0)
            pass_on(("B", 0, 0, 1))
            pass_on(("A", 0, 0, 1))
            step_spread()
            continue
        item, bank = item[:4], item[4]
        receive(item, bank)
        if not bank:
            pass_on(item)
        key = (item[0], bank, item[2])
        have[key] = have.get(key, 2 * int(item[2] == 0 and not bank)) + 1
        if have[key] == 4:
            ready[item[0]].append((bank, item[2]))
        if state["weights"]:
            for color in "AB":
                if sizes[color] and len(ready[color]) >= sizes[color][0]:
                    compute(color, [ready[color].pop(0) for _ in range(sizes[color].pop(0))])
                    break
    for color in "AB":
        for size in sizes[color]:
            compute(color, [ready[color].pop(0) for _ in range(size)])

    back = {}
    for i in (2, 0, 1):
        rows = pl.ds(i * hidden, hidden)
        made_here[i * hidden : (i + 1) * hidden, :] = acc[i * hidden : (i + 1) * hidden, :].astype(BF16)
        copy = remote(made_here.at[rows], made_there.at[rows], ret_s.at[i], ret_r.at[i], (sibling, z * NX + across))
        back[i] = copy

        @pl.when(role == 1)
        def _():
            copy.start()

    waits["m2"]()
    outs = [
        pltpu.make_async_copy(moments.at[pl.ds(0, hidden)], wdn_out, out_sem.at[0]),
        pltpu.make_async_copy(moments.at[pl.ds(hidden, hidden)], mom1_out, out_sem.at[1]),
        pltpu.make_async_copy(moments.at[pl.ds(2 * hidden, hidden)], mom2_out, out_sem.at[2]),
    ]
    for copy in outs:
        copy.start()
    for copy in pending:
        copy.wait_send()

    def result(made, i):
        goal = dgrad_out if i == 2 else gin_out.at[pl.ds(i * hidden, hidden)]
        return pltpu.make_async_copy(made.at[pl.ds(i * hidden, hidden)], goal, out_sem.at[3 + i])

    @pl.when(role == 0)
    def _():
        for i in (2, 0, 1):
            result(made_here, i).start()

    @pl.when(role == 1)
    def _():
        for copy in pending_far:
            copy.wait_send()
        for i in (2, 0, 1):
            back[i].wait()
            result(made_there, i).start()

    for copy in outs + [result(made_here, i) for i in range(3)]:
        copy.wait()


def local(tokens, grad_out, route_weights, expert_ids, swap_code, w_in, w_down, moment1, moment2):
    width = tokens.shape[1]
    hidden = w_down.shape[1]
    vmem, anywhere = pltpu.VMEM, pl.BlockSpec(memory_space=pl.ANY)
    half_w, quarter = 3 * hidden // 2, width // 4
    half_m = half_w
    dma = pltpu.SemaphoreType.DMA
    gin, dgrad, wdn, mom1, mom2 = pl.pallas_call(
        kernel,
        out_shape=(
            jax.ShapeDtypeStruct((2 * hidden, width), BF16),
            jax.ShapeDtypeStruct((hidden, width), BF16),
            jax.ShapeDtypeStruct((hidden, width), BF16),
            jax.ShapeDtypeStruct((hidden, width), BF16),
            jax.ShapeDtypeStruct((hidden, width), BF16),
        ),
        in_specs=[
            pl.BlockSpec(memory_space=pltpu.VMEM),
            pl.BlockSpec(memory_space=pltpu.VMEM),
            pl.BlockSpec(memory_space=pltpu.SMEM),
        ]
        + [anywhere] * 6,
        out_specs=(anywhere,) * 5,
        scratch_shapes=[
            vmem(tokens.shape, BF16),
            vmem(tokens.shape, BF16),
            vmem((2, hidden, width), F32),
            vmem((16 * NE, tokens.shape[0]), BF16),
            vmem((16 * NE, tokens.shape[0]), BF16),
            vmem((16 * NE, 1), F32),
            vmem((NE, tokens.shape[0]), F32),
            vmem((NE, 16, width), BF16),
            vmem((NE, 16, width), BF16),
            vmem((2, NZ, 2, ROWS_A, width), BF16),
            vmem((2, NZ, 2, ROWS_B, width), BF16),
            vmem((5 * hidden, width), BF16),
            vmem((NE, half_w, quarter), BF16),
            vmem((NE, half_m, quarter), BF16),
            vmem((NE, half_w, quarter), BF16),
            vmem((NE, half_m, quarter), BF16),
            vmem((4 * hidden, width), BF16),
            vmem((width, 4 * hidden), BF16),
            vmem((3 * hidden, width), BF16),
            vmem((4 * hidden, width), F32),
            vmem((3 * hidden, width), BF16),
            vmem((3 * hidden, width), BF16),
            dma((7,)), dma((6,)), dma((3,)),
            dma((2, NE)), dma((2, NE)), dma((NE,)), dma((NE,)), dma((NE,)),
            dma((NE,)), dma((NE,)), dma((NE,)), dma((NE,)), dma((NE,)),
            dma((2, 2, 2 * NZ)), dma((2, 2, 2 * NZ)), dma((N_SENDS,)), dma((3,)), dma((3,)),
        ],
        compiler_params=pltpu.CompilerParams(
            collective_id=0, has_side_effects=True, vmem_limit_bytes=60 << 20
        ),
    )(expert_ids.T, route_weights.T, swap_code, tokens, grad_out, w_in, w_down, moment1, moment2)
    steps = 2
    thin = pl.BlockSpec((hidden // steps, width), lambda i: (i, 0))
    thick = pl.BlockSpec((2 * hidden // steps, width), lambda i: (i, 0))
    down_new, first_new, second_new, in_new = pl.pallas_call(
        adam,
        grid=(steps,),
        out_shape=(
            jax.ShapeDtypeStruct((hidden, width), BF16),
            jax.ShapeDtypeStruct((hidden, width), F32),
            jax.ShapeDtypeStruct((hidden, width), F32),
            jax.ShapeDtypeStruct((2 * hidden, width), BF16),
        ),
        in_specs=[thick, thin, thin, thin, thin],
        out_specs=(thin, thin, thin, thick),
        compiler_params=pltpu.CompilerParams(vmem_limit_bytes=60 << 20),
    )(gin, dgrad, wdn, mom1, mom2)
    return down_new[None], first_new[None], second_new[None], in_new.reshape(1, 2, hidden, width)


def adam(gin, dgrad, wdn, mom1, mom2, down_new, first_new, second_new, in_new):
    grad = dgrad[...].astype(F32)
    first = BETA_ONE * mom1[...].astype(F32) + (1.0 - BETA_ONE) * grad
    second = BETA_TWO * mom2[...].astype(F32) + (1.0 - BETA_TWO) * (grad * grad)
    fix_one = 1.0 - BETA_ONE**ADAM_STEP
    fix_two = 1.0 - BETA_TWO**ADAM_STEP
    step_size = first * (1.0 / fix_one) / (jnp.sqrt(second * (1.0 / fix_two)) + ADAM_EPS)
    down_new[...] = (wdn[...].astype(F32) - ADAM_RATE * step_size).astype(BF16)
    first_new[...] = first
    second_new[...] = second
    in_new[...] = gin[...]


def solution(mesh):
    rows = P(("expert", "dp"), None)
    wide = P("expert", None, "dp", None)
    slot = P("expert", "dp", None)
    return jax.shard_map(
        local,
        mesh=mesh,
        in_specs=(rows, rows, rows, rows, P(), wide, slot, slot, slot),
        out_specs=(slot, slot, slot, wide),
        check_vma=False,
    )
```
